256 devices in a mesh: seq: 128 (over z, x_hi, y, core), head: 2 (over x_lo).
Axes of the slice: x: 4 (x_hi: 2, x_lo: 2; x = x_hi * 2 + x_lo), y: 4, z: 8, core: 2. Of those that a mesh axis runs over, the one named last changes fastest.
Arguments:
- query: bfloat16 [32768, 8, 4, 128], P('seq', None, 'head'), may hold values from -40 to 40
- key_in: bfloat16 [32768, 8, 128], P('seq', 'head'), may hold values from -16 to 16
- value: bfloat16 [32768, 8, 128], P('seq', 'head'), may hold values from -6 to 6
- grad_out: bfloat16 [32768, 8, 4, 128], P('seq', None, 'head'), may hold values from -6 to 6
- band_width: int32 [8, 4], P(None, 'head'), may hold values from 1 to 2, as said below
- stride_bits: int32 [7], replicated, may hold values from 0 to 6, each once
- partner_table: int32 [256, 7], P('seq'), may hold values from 0 to 1
Outputs:
- attn_out: bfloat16 [32768, 8, 4, 128], P('seq', None, 'head')
- grad_query: bfloat16 [32768, 8, 4, 128], P('seq', None, 'head')
- grad_key: bfloat16 [32768, 8, 128], P('seq', 'head')
- grad_value: bfloat16 [32768, 8, 128], P('seq', 'head')
The draws below stay inside these ranges and needn't reach their ends.
Inputs may be any that keep to these rules, and one draw needn't show every extreme that they name: `band_width`: some query head has band width 1 and some has 2. `stride_bits`: each section flips a different bit.
All inputs are finite; a program needn't handle non-finite values.
Results may differ from the reference program's by a relative error of at most 0.023.
Values may be sent and summed in bfloat16 or wider, within the bound.
No kernel may reach another device: no remote copies, remote signals or barrier semaphores. Data moves between devices by JAX's collectives and lax.ppermute only.
A program may use at most 192 MiB of HBM per device.

```python
import jax
import jax.numpy as jnp
from jax import lax

HD = 128
KVH = 8
GROUP = 4
BLOCK = 128
BANDMAX = 2
TOK_DEV = 256
TOKENS = 32768
LEVELS = 7
NB = 256


def pair_draw(key):
    query_seed = jax.random.fold_in(key, 101)
    key_seed = jax.random.fold_in(key, 102)
    query_rows = jax.random.normal(query_seed, (TOKENS, KVH, GROUP, HD), jnp.float32)
    key_rows = jax.random.normal(key_seed, (TOKENS, KVH, HD), jnp.float32)
    return (jnp.clip(query_rows, -40.0, 40.0), jnp.clip(key_rows, -16.0, 16.0))


def draw_query(key, part):
    return pair_draw(key)[0].astype(jnp.bfloat16)


def draw_key_in(key, part):
    return pair_draw(key)[1].astype(jnp.bfloat16)


def draw_band_width(key, part):
    count = KVH * GROUP
    order = jax.random.permutation(jax.random.fold_in(key, 201), count)
    rough = jax.random.randint(jax.random.fold_in(key, 202), (count,), 1, BANDMAX + 1)
    widths = jnp.where(order == 0, 1, jnp.where(order == 1, BANDMAX, rough))
    return widths.reshape(KVH, GROUP).astype(jnp.int32)


def touch_ends(result, own_key, low, high):
    extent = result.shape
    index_at = [jax.random.randint(jax.random.fold_in(own_key, axis), (), 0, extent[axis]) for axis in range(len(extent))]
    result = result.at[tuple(index_at)].set(low)
    longest = extent.index(max(extent))
    index_at[longest] = (index_at[longest] + 1) % extent[longest]
    return result.at[tuple(index_at)].set(high)


def shard_levels(stream_key, dims, pieces, low, top_value):
    def one(position, blocks):
        draws = jax.random.uniform(jax.random.fold_in(jax.random.fold_in(stream_key, 6), position), (blocks,), jnp.float32, low / len(pieces), top_value / len(pieces))
        return jnp.repeat(jnp.exp(draws), dims[position] // blocks).reshape((-1,) + (1,) * (len(dims) - position - 1))

    gain = one(*pieces[0])
    for cut in pieces[1:]:
        gain = gain * one(*cut)
    return gain


def centred(own_key, extent, deviation, bound, cuts=(), kind=jnp.bfloat16):
    array = deviation * jax.random.normal(own_key, extent, jnp.float32)
    if cuts:
        array = array * shard_levels(own_key, extent, cuts, -0.22, 0.18)
    return jnp.clip(array, -bound, bound).astype(kind)


def setup_inputs(seed: int = 0) -> dict:
    seeds = jax.random.split(jax.random.key(seed), 8)
    query = draw_query(jax.random.fold_in(seeds[7], 71), 0)
    key_in = draw_key_in(jax.random.fold_in(seeds[7], 71), 0)
    value = centred(seeds[2], (TOKENS, KVH, HD), 1.0, 6.0, ((0, 128), (1, 2)))
    grad_out = centred(seeds[3], (TOKENS, KVH, GROUP, HD), 1.0, 6.0, ((0, 128), (2, 2)))
    band_width = draw_band_width(jax.random.fold_in(seeds[7], 71), 0)
    stride_bits = jax.random.permutation(seeds[5], LEVELS).astype(jnp.int32)
    partner_table = touch_ends(jax.random.randint(seeds[6], (NB, LEVELS), 0, TOK_DEV // BLOCK), jax.random.fold_in(seeds[6], 1), 0, (TOK_DEV // BLOCK) - 1).astype(jnp.int32)
    return dict(query=query, key_in=key_in, value=value, grad_out=grad_out, band_width=band_width, stride_bits=stride_bits, partner_table=partner_table)


def reference(query, key_in, value, grad_out, band_width, stride_bits, partner_table):
    tokens = query.shape[0]
    kv_heads = key_in.shape[1]
    groups = query.shape[2]
    head_dim = query.shape[3]
    all_blocks = tokens // BLOCK
    local_blocks = TOK_DEV // BLOCK
    half_band = BANDMAX - 1
    levels = stride_bits.shape[0]
    score_scale = head_dim ** -0.5
    blocks = jnp.arange(all_blocks, dtype=jnp.int32)
    offsets = jnp.arange(-half_band, half_band + 1, dtype=jnp.int32)
    band_index = blocks[:, None] + offsets[None, :]
    edge_valid = (band_index >= 0) & (band_index < all_blocks)
    owner_device = blocks // local_blocks
    flips = jnp.left_shift(jnp.int32(1), stride_bits.astype(jnp.int32))
    partner_device = jnp.bitwise_xor(owner_device[:, None], flips[None, :])
    partner_index = (partner_device * local_blocks + partner_table).astype(jnp.int32)
    key_index = jnp.concatenate([jnp.clip(band_index, 0, all_blocks - 1), partner_index], axis=1).astype(jnp.int32)
    width_valid = jnp.abs(offsets)[None, None, :] < band_width[:, :, None]
    key_blocks = key_in.reshape(all_blocks, BLOCK, kv_heads, head_dim)
    value_blocks = value.reshape(all_blocks, BLOCK, kv_heads, head_dim)

    def block_step(totals, block_num):
        grad_keys, grad_values = totals
        block_list = key_index[block_num]
        key_rows = key_blocks[block_list].reshape(-1, kv_heads, head_dim).astype(jnp.float32)
        value_rows = value_blocks[block_list].reshape(-1, kv_heads, head_dim).astype(jnp.float32)
        start = (block_num * BLOCK).astype(jnp.int32)
        query_rows = lax.dynamic_slice_in_dim(query, start, BLOCK, 0).astype(jnp.float32)
        grad_rows = lax.dynamic_slice_in_dim(grad_out, start, BLOCK, 0).astype(jnp.float32)
        band_valid = width_valid & edge_valid[block_num][None, None, :]
        valid_keys = jnp.concatenate([band_valid, jnp.ones((kv_heads, groups, levels), jnp.bool_)], axis=-1)
        valid_keys = jnp.repeat(valid_keys, BLOCK, axis=-1)
        scores = jnp.einsum('qhgd,khd->hgqk', query_rows, key_rows) * score_scale
        scores = jnp.where(valid_keys[:, :, None, :], scores, -jnp.inf)
        row_max = jnp.max(scores, axis=-1, keepdims=True)
        log_total = row_max + jnp.log(jnp.sum(jnp.exp(scores - row_max), axis=-1, keepdims=True))
        probability = jnp.exp(scores - log_total)
        weights = probability.astype(jnp.bfloat16).astype(jnp.float32)
        output = jnp.einsum('hgqk,khd->qhgd', weights, value_rows).astype(jnp.bfloat16)
        row_delta = jnp.sum(grad_rows * output.astype(jnp.float32), axis=-1)
        grad_prob = jnp.einsum('qhgd,khd->hgqk', grad_rows, value_rows)
        grad_score = (probability * (grad_prob - jnp.transpose(row_delta, (1, 2, 0))[..., None])).astype(jnp.bfloat16).astype(jnp.float32)
        grad_q = (jnp.einsum('hgqk,khd->qhgd', grad_score, key_rows) * score_scale).astype(jnp.bfloat16)
        grad_k = jnp.einsum('hgqk,qhgd->khd', grad_score, query_rows) * score_scale
        grad_v = jnp.einsum('hgqk,qhgd->khd', weights, grad_rows)
        grad_keys = grad_keys.at[block_list].add(grad_k.reshape(-1, BLOCK, kv_heads, head_dim))
        grad_values = grad_values.at[block_list].add(grad_v.reshape(-1, BLOCK, kv_heads, head_dim))
        return (grad_keys, grad_values), (output, grad_q)

    zero_grads = jnp.zeros((all_blocks, BLOCK, kv_heads, head_dim), jnp.float32)
    (grad_keys, grad_values), (outputs, grad_queries) = lax.scan(block_step, (zero_grads, zero_grads), blocks)
    return (outputs.reshape(query.shape), grad_queries.reshape(query.shape),
            grad_keys.reshape(key_in.shape).astype(jnp.bfloat16), grad_values.reshape(value.shape).astype(jnp.bfloat16))
```

```python
import math

import jax
import jax.numpy as jnp
from jax import lax
from jax.experimental import pallas as pl
from jax.experimental.pallas import tpu as pltpu
from jax.sharding import PartitionSpec as P

BLOCK = 128
HEAD_DIM = 128
CHUNKS = 1
LOCAL_HEADS = 4
LEVELS = 7
BAND_SLOTS = 3
SLOTS = BAND_SLOTS + LEVELS
ROWS = 512
NEG = -1e30
F32 = jnp.float32
BF16 = jnp.bfloat16
WHOLE = pl.BlockSpec(memory_space=pltpu.VMEM)
SCALARS = pl.BlockSpec(memory_space=pltpu.SMEM)


def vmem(mib):
    return pltpu.CompilerParams(vmem_limit_bytes=mib << 20)


def dot(lhs, rhs, lhs_dim, rhs_dim):
    return lax.dot_general(
        lhs, rhs, (((lhs_dim,), (rhs_dim,)), ((), ())), preferred_element_type=F32
    )


def query_order(place, rows_first):
    ordered = lax.broadcasted_iota(jnp.int32, (256, 256), rows_first)
    natural = lax.broadcasted_iota(jnp.int32, (256, 256), 1 - rows_first)
    source = (ordered & 15) * 16 + ((ordered >> 4) ^ (place * 8))
    return (natural == source).astype(BF16)


def key_order(rows_first):
    ordered = lax.broadcasted_iota(jnp.int32, (256, 256), rows_first)
    natural = lax.broadcasted_iota(jnp.int32, (256, 256), 1 - rows_first)
    return (natural == (ordered & 63) * 4 + (ordered >> 6)).astype(BF16)


def pack_kernel(scalars, query, grad, key, value, *outs):
    place = scalars[0]
    chunks = len(outs) // 3
    pairs, keeps, sends = outs[:chunks], outs[chunks : 2 * chunks], outs[2 * chunks :]
    per = LOCAL_HEADS // chunks
    order = key_order(0)
    for member, source in enumerate((key, value)):
        for part in range(4):
            rows = dot(order, source[part * 256 : part * 256 + 256], 1, 0).astype(BF16)
            for head in range(LOCAL_HEADS):
                pairs[head // per][head % per, member, part * 64 : part * 64 + 64] = rows[
                    head * 64 : head * 64 + 64
                ]
    order = query_order(place, 0)
    for member, source in enumerate((query, grad)):
        for part in range(16):
            rows = dot(order, source[part * 256 : part * 256 + 256], 1, 0).astype(BF16)
            block, inner = part // 8, (part % 8) * 16
            for head in range(2 * LOCAL_HEADS):
                target = (keeps, sends)[head // LOCAL_HEADS]
                local = head % LOCAL_HEADS
                for group in range(2):
                    start = (member * 2 + block) * 256 + group * 128 + inner
                    first = (head * 2 + group) * 16
                    target[local // per][local % per, start : start + 16] = rows[first : first + 16]
    sublane = lax.broadcasted_iota(jnp.int32, (16, HEAD_DIM), 0)
    for head in range(2 * LOCAL_HEADS):
        target = (keeps, sends)[head // LOCAL_HEADS]
        local = head % LOCAL_HEADS
        actual = head ^ (place * LOCAL_HEADS)
        width = jnp.where(sublane == 0, scalars[1 + actual * 2], scalars[2 + actual * 2])
        target[local // per][local % per, 1024:1040] = width.astype(F32).astype(BF16)


def attend_kernel(scalars, *refs):
    own, ext = refs[0], refs[1]
    arrived = refs[2 : 2 + LEVELS]
    keep, other = refs[2 + LEVELS : 4 + LEVELS]
    outs = refs[4 + LEVELS :]
    keep_out, other_out, own_out, ext_out = outs[:4]
    level_out = outs[4 : 4 + LEVELS]
    scores, exps, dscores, keys, values, acc = outs[4 + LEVELS :]
    heads = own.shape[0]
    device = scalars[0]
    last = scalars[1]
    even = (device & 1) == 0
    scale = HEAD_DIM**-0.5
    log_scale = scale * math.log2(math.e)

    def one_head(head, carry):
        acc[...] = jnp.zeros_like(acc)
        widths = jnp.concatenate(
            [
                ref[head, 1024:1040].astype(F32)[group : group + 1]
                for ref in (keep, other)
                for group in range(2)
            ],
            axis=1,
        )
        width_bias = jnp.where(widths > 1.5, 0.0, NEG)
        for block in range(2):
            side = 1 - block
            outer_valid = device > 0 if block == 0 else device < last
            from_ext = even if block == 0 else jnp.logical_not(even)
            side_rows = side * BLOCK
            for member, store in enumerate((keys, values)):
                store[0:BLOCK] = own[head, member, 0:BLOCK]
                store[BLOCK : 2 * BLOCK] = own[head, member, BLOCK : 2 * BLOCK]
                store[2 * BLOCK : 3 * BLOCK] = jnp.where(
                    from_ext,
                    ext[head, member],
                    arrived[0][head, member, side_rows : side_rows + BLOCK],
                )
                for level in range(LEVELS):
                    chosen = scalars[2 + block * LEVELS + level]
                    first = (BAND_SLOTS + level) * BLOCK
                    store[first : first + BLOCK] = arrived[level][
                        head, member, pl.ds(pl.multiple_of(chosen * BLOCK, BLOCK), BLOCK)
                    ]
            query_t, grad_t = (
                jnp.concatenate(
                    [
                        jnp.transpose(
                            ref[
                                head,
                                (member * 2 + block) * 256 : (member * 2 + block) * 256 + 256,
                            ]
                        )
                        for ref in (keep, other)
                    ],
                    axis=1,
                )
                for member in range(2)
            )
            outer_bias = width_bias + jnp.where(outer_valid, 0.0, NEG)
            peak = jnp.full((8, ROWS), NEG, F32)
            for slot in range(SLOTS):
                span = slice(slot * BLOCK, slot * BLOCK + BLOCK)
                part = dot(keys[span], query_t, 1, 0)
                if slot == side:
                    part = part + width_bias
                if slot == 2:
                    part = part + outer_bias
                scores[span] = part
                peak = jnp.maximum(peak, jnp.max(part.reshape(BLOCK // 8, 8, ROWS), axis=0))
            peak = jnp.max(peak, axis=0, keepdims=True) * log_scale
            total = jnp.zeros((8, ROWS), F32)
            for slot in range(SLOTS):
                span = slice(slot * BLOCK, slot * BLOCK + BLOCK)
                part = jnp.exp2(scores[span] * log_scale - peak)
                total = total + jnp.sum(part.reshape(BLOCK // 8, 8, ROWS), axis=0)
                exps[span] = part.astype(BF16)
            inverse = 1.0 / jnp.sum(total, axis=0, keepdims=True)
            out_t = (dot(values[...], exps[...], 0, 0) * inverse).astype(BF16)
            grad_t = (grad_t.astype(F32) * inverse).astype(BF16)
            delta = jnp.sum(out_t.astype(F32) * grad_t.astype(F32), axis=0, keepdims=True)
            for slot in range(SLOTS):
                span = slice(slot * BLOCK, slot * BLOCK + BLOCK)
                part = dot(values[span], grad_t, 1, 0)
                dscores[span] = (exps[span].astype(F32) * (part - delta)).astype(BF16)
            dquery_t = (dot(keys[...], dscores[...], 0, 0) * scale).astype(BF16)
            for member, rows_t in enumerate((out_t, dquery_t)):
                first = (member * 2 + block) * 256
                keep_out[head, first : first + 256] = jnp.transpose(rows_t[:, 0:256])
                other_out[head, first : first + 256] = jnp.transpose(rows_t[:, 256:512])
            outer_row = jnp.where(from_ext, 2, 3 + side)
            for member, (lhs, rhs, factor) in enumerate(
                ((dscores, query_t, scale), (exps, grad_t, None))
            ):
                terms = dot(lhs[...], rhs, 1, 1)
                if factor is not None:
                    terms = terms * factor
                acc[member, 0 : 2 * BLOCK] += terms[0 : 2 * BLOCK]
                targets = [outer_row] + [
                    3 + 2 * level + scalars[2 + block * LEVELS + level] for level in range(LEVELS)
                ]
                for slot, row in enumerate(targets):
                    at = pl.ds(pl.multiple_of(row * BLOCK, BLOCK), BLOCK)
                    first = (2 + slot) * BLOCK
                    acc[member, at] += terms[first : first + BLOCK]
        for member in range(2):
            own_out[head, member] = acc[member, 0 : 2 * BLOCK]
            ext_out[head, member] = acc[member, 2 * BLOCK : 3 * BLOCK].astype(BF16)
            for level in range(LEVELS):
                first = (3 + 2 * level) * BLOCK
                level_out[level][head, member] = acc[member, first : first + 2 * BLOCK].astype(BF16)
        return carry

    lax.fori_loop(0, heads, one_head, 0)


def finish_kernel(scalars, *refs):
    place, even = scalars[0], scalars[1]
    ins, outs = refs[:-4], refs[-4:]
    out_ref, dquery_ref, dkey_ref, dvalue_ref = outs
    per_chunk = len(ins) // CHUNKS
    per = LOCAL_HEADS // CHUNKS
    order = query_order(place, 1)
    for member, target in enumerate((out_ref, dquery_ref)):
        for part in range(16):
            block, inner = part // 8, (part % 8) * 16
            pieces = []
            for head in range(2 * LOCAL_HEADS):
                local = head % LOCAL_HEADS
                source = ins[(local // per) * per_chunk + head // LOCAL_HEADS]
                for group in range(2):
                    start = (member * 2 + block) * 256 + group * 128 + inner
                    pieces.append(source[local % per, start : start + 16])
            rows = jnp.concatenate(pieces, axis=0)
            target[part * 256 : part * 256 + 256] = dot(order, rows, 1, 0).astype(BF16)
    order = key_order(1)
    for member, target in enumerate((dkey_ref, dvalue_ref)):
        for part in range(4):
            pieces = []
            for head in range(LOCAL_HEADS):
                mine = ins[(head // per) * per_chunk : (head // per + 1) * per_chunk]
                span = slice(part * 64, part * 64 + 64)
                total = mine[2][head % per, member, span]
                for ref in mine[4:]:
                    total = total + ref[head % per, member, span].astype(F32)
                inner = (part % 2) * 64
                beyond = mine[3][head % per, member, inner : inner + 64].astype(F32)
                here = even == 1 if part < 2 else even == 0
                total = total + jnp.where(here, beyond, 0.0)
                pieces.append(total.astype(BF16))
            rows = jnp.concatenate(pieces, axis=0)
            target[part * 256 : part * 256 + 256] = dot(order, rows, 1, 0).astype(BF16)


def flipped(value, mask):
    return lax.ppermute(value, "seq", [(i, i ^ mask) for i in range(lax.axis_size("seq"))])


def past_end(value):
    pairs = []
    for i in range(1, lax.axis_size("seq") - 1, 2):
        pairs += [(i, i + 1), (i + 1, i)]
    return lax.ppermute(value, "seq", pairs)


def other_head(value):
    return lax.ppermute(value, "head", [(0, 1), (1, 0)])


def shards(query, key_in, value, grad_out, band_width, stride_bits, partner_table):
    rows = key_in.shape[0]
    per = LOCAL_HEADS // CHUNKS
    device = lax.axis_index("seq").astype(jnp.int32)
    place = lax.axis_index("head").astype(jnp.int32)
    even = (device & 1) == 0
    match = (stride_bits[None, :] == jnp.arange(LEVELS, dtype=jnp.int32)[:, None]).astype(jnp.int32)
    chosen = jnp.sum(partner_table[:, None, :] * match[None], axis=2)

    pair = jax.ShapeDtypeStruct((per, 2, rows, HEAD_DIM), BF16)
    sides = jax.ShapeDtypeStruct((per, 1040, HEAD_DIM), BF16)
    packed = pl.pallas_call(
        pack_kernel,
        out_shape=[pair] * CHUNKS + [sides] * (2 * CHUNKS),
        in_specs=[SCALARS] + [WHOLE] * 4,
        out_specs=[WHOLE] * (3 * CHUNKS),
        compiler_params=vmem(24),
        name="pack",
    )(
        jnp.concatenate([place[None], band_width.reshape(-1)]),
        query.reshape(-1, HEAD_DIM),
        grad_out.reshape(-1, HEAD_DIM),
        key_in.reshape(-1, HEAD_DIM),
        value.reshape(-1, HEAD_DIM),
    )
    pairs, keeps, sends = packed[:CHUNKS], packed[CHUNKS : 2 * CHUNKS], packed[2 * CHUNKS :]

    scalars = jnp.concatenate(
        [device[None], jnp.full((1,), lax.axis_size("seq") - 1, jnp.int32), chosen.reshape(-1)]
    )
    end = jax.ShapeDtypeStruct((per, 2, BLOCK, HEAD_DIM), BF16)
    half = jax.ShapeDtypeStruct((per, 1024, HEAD_DIM), BF16)
    parts = []
    for chunk in range(CHUNKS):
        own = pairs[chunk]
        arrived = [None] * LEVELS
        arrived[5] = flipped(own, 32)
        arrived[1] = flipped(own, 2)
        arrived[3] = flipped(own, 8)
        other = other_head(sends[chunk])
        arrived[6] = flipped(arrived[5], 96)
        arrived[4] = flipped(own, 16)
        arrived[2] = flipped(arrived[1], 6)
        ends = jnp.where(even, own[:, :, :BLOCK], own[:, :, BLOCK:])
        ext = past_end(ends)
        arrived[0] = flipped(own, 1)
        results = pl.pallas_call(
            attend_kernel,
            out_shape=[
                half,
                half,
                jax.ShapeDtypeStruct((per, 2, rows, HEAD_DIM), F32),
                end,
            ]
            + [pair] * LEVELS,
            in_specs=[SCALARS] + [WHOLE] * (4 + LEVELS),
            out_specs=[WHOLE] * (4 + LEVELS),
            scratch_shapes=[
                pltpu.VMEM((SLOTS * BLOCK, ROWS), F32),
                pltpu.VMEM((SLOTS * BLOCK, ROWS), BF16),
                pltpu.VMEM((SLOTS * BLOCK, ROWS), BF16),
                pltpu.VMEM((SLOTS * BLOCK, HEAD_DIM), BF16),
                pltpu.VMEM((SLOTS * BLOCK, HEAD_DIM), BF16),
                pltpu.VMEM((2, (3 + 2 * LEVELS) * BLOCK, HEAD_DIM), F32),
            ],
            compiler_params=vmem(40),
            name="attend",
        )(scalars, own, ext, *arrived, keeps[chunk], other)
        keep_out, other_out, own_terms, ext_terms = results[:4]
        terms = results[4:]
        far = flipped(terms[6], 96)
        near = flipped(terms[2], 6)
        swapped_out = other_head(other_out)
        back = [
            flipped(terms[4], 16),
            flipped(terms[3], 8),
            flipped((terms[5].astype(F32) + far.astype(F32)).astype(BF16), 32),
            flipped((terms[1].astype(F32) + near.astype(F32)).astype(BF16), 2),
            flipped(terms[0], 1),
        ]
        ext_back = past_end(ext_terms)
        parts += [keep_out, swapped_out, own_terms, ext_back] + back

    results = pl.pallas_call(
        finish_kernel,
        out_shape=[jax.ShapeDtypeStruct((rows * 16, HEAD_DIM), BF16)] * 2
        + [jax.ShapeDtypeStruct((rows * 4, HEAD_DIM), BF16)] * 2,
        in_specs=[SCALARS] + [WHOLE] * len(parts),
        out_specs=[WHOLE] * 4,
        compiler_params=vmem(32),
        name="finish",
    )(jnp.stack([place, even.astype(jnp.int32)]), *parts)
    return (
        results[0].reshape(query.shape),
        results[1].reshape(query.shape),
        results[2].reshape(key_in.shape),
        results[3].reshape(key_in.shape),
    )


def solution(mesh):
    placed = (
        P("seq", None, "head", None),
        P("seq", "head", None),
        P("seq", "head", None),
        P("seq", None, "head", None),
        P(None, "head"),
        P(),
        P("seq", None),
    )
    return jax.shard_map(
        shards,
        mesh=mesh,
        in_specs=placed,
        out_specs=(
            P("seq", None, "head", None),
            P("seq", None, "head", None),
            P("seq", "head", None),
            P("seq", "head", None),
        ),
        check_vma=False,
    )
```

```python
import functools
import math

import jax
import jax.numpy as jnp
from jax import lax
from jax.experimental import pallas as pl
from jax.experimental.pallas import tpu as pltpu
from jax.sharding import PartitionSpec as P

BLOCK = 128
HEAD_DIM = 128
CHUNKS = 2
LOCAL_HEADS = 4
PER = LOCAL_HEADS // CHUNKS
LEVELS = 7
BAND_SLOTS = 3
SLOTS = BAND_SLOTS + LEVELS
ROWS = 512
PAD = 8
PACK_MIB = 56
SIDES_MIB = 52
NEG = -1e30
F32 = jnp.float32
BF16 = jnp.bfloat16
WHOLE = pl.BlockSpec(memory_space=pltpu.VMEM)
FAR = pl.BlockSpec(memory_space=pltpu.HBM)
SCALARS = pl.BlockSpec(memory_space=pltpu.SMEM)


def vmem(mib):
    return pltpu.CompilerParams(vmem_limit_bytes=mib << 20)


def dot(lhs, rhs, lhs_dim, rhs_dim):
    return lax.dot_general(
        lhs, rhs, (((lhs_dim,), (rhs_dim,)), ((), ())), preferred_element_type=F32
    )


def query_order(place, rows_first):
    ordered = lax.broadcasted_iota(jnp.int32, (256, 256), rows_first)
    natural = lax.broadcasted_iota(jnp.int32, (256, 256), 1 - rows_first)
    source = (ordered & 15) * 16 + ((ordered >> 4) ^ (place * 8))
    return (natural == source).astype(BF16)


def key_order(rows_first):
    ordered = lax.broadcasted_iota(jnp.int32, (256, 256), rows_first)
    natural = lax.broadcasted_iota(jnp.int32, (256, 256), 1 - rows_first)
    return (natural == (ordered & 63) * 4 + (ordered >> 6)).astype(BF16)


def pieces_of(ref, store, sems, count):
    rows = ref.shape[0] // count
    copies = [
        pltpu.make_async_copy(
            ref.at[pl.ds(i * rows, rows)], store.at[pl.ds(i * rows, rows)], sems.at[i]
        )
        for i in range(count)
    ]
    for copy in copies:
        copy.start()
    return copies


def pack_pairs_kernel(scalars, key, value, *refs):
    whole, first, second, ends, key_in, value_in, sems = refs
    even = scalars[0] == 0
    copies = [
        pieces_of(ref, store, sems.at[member], 2)
        for member, (ref, store) in enumerate(((key, key_in), (value, value_in)))
    ]
    order = key_order(0)
    for block in range(2):
        for member, store in enumerate((key_in, value_in)):
            copies[member][block].wait()
            for inner in (0, 64):
                start = block * 512 + inner * 4
                rows = dot(order, store[start : start + 256], 1, 0).astype(BF16)
                span = slice(block * BLOCK + inner, block * BLOCK + inner + 64)
                end = slice(inner, inner + 64)
                for head in range(LOCAL_HEADS):
                    piece = rows[head * 64 : head * 64 + 64]
                    whole[head, member, span] = piece
                    (first, second)[head // PER][head % PER, member, span] = piece
                    if block == 0:
                        ends[head, member, end] = piece
                    else:
                        ends[head, member, end] = jnp.where(even, ends[head, member, end], piece)


def pack_sides_kernel(scalars, query, grad, unused, *refs):
    place = scalars[0]
    keeps, sends = refs[:CHUNKS], refs[CHUNKS : 2 * CHUNKS]
    stores, sems = refs[2 * CHUNKS : 2 * CHUNKS + 2], refs[2 * CHUNKS + 2]
    copies = [
        pieces_of(ref, store, sems.at[member], 4)
        for member, (ref, store) in enumerate(zip((query, grad), stores))
    ]
    order = query_order(place, 0)
    for part in range(16):
        for member, store in enumerate(stores):
            if part % 4 == 0:
                copies[member][part // 4].wait()
            rows = dot(order, store[part * 256 : part * 256 + 256], 1, 0).astype(BF16)
            block, inner = part // 8, (part % 8) * 16
            for head in range(2 * LOCAL_HEADS):
                target = (keeps, sends)[head // LOCAL_HEADS]
                local = head % LOCAL_HEADS
                for group in range(2):
                    start = (member * 2 + block) * 256 + group * 128 + inner
                    first = (head * 2 + group) * 16
                    target[local // PER][local % PER, start : start + 16] = rows[first : first + 16]
    sublane = lax.broadcasted_iota(jnp.int32, (16, HEAD_DIM), 0)
    for head in range(2 * LOCAL_HEADS):
        target = (keeps, sends)[head // LOCAL_HEADS]
        local = head % LOCAL_HEADS
        actual = head ^ (place * LOCAL_HEADS)
        width = jnp.where(sublane == 0, scalars[1 + actual * 2], scalars[2 + actual * 2])
        target[local // PER][local % PER, 1024:1040] = width.astype(F32).astype(BF16)


def attend_kernel(base, reused, scalars, *refs):
    own, ext = refs[:2]
    arrived = refs[2 : 2 + LEVELS]
    sides = refs[2 + LEVELS : 4 + LEVELS]
    refs = refs[4 + LEVELS + reused :]
    side_outs, terms_out, ext_out = refs[:2], refs[2], refs[3]
    level_outs = refs[4 : 4 + LEVELS]
    (scores, exps, dscores, pairs, side_in, side_store, acc, ext_store, level_store) = refs[
        4 + LEVELS : 13 + LEVELS
    ]
    pair_sems, side_sems, out_sems = refs[13 + LEVELS :]
    device = scalars[0]
    last = scalars[1]
    even = (device & 1) == 0
    odd = jnp.logical_not(even)
    scale = HEAD_DIM**-0.5
    log_scale = scale * math.log2(math.e)

    def chosen(block, level):
        return scalars[2 + block * LEVELS + level]

    def at_head(ref, head):
        return ref.at[head + base if ref.shape[0] == LOCAL_HEADS else head]

    def copy_pair(head, block, source, slot, count):
        unit = head * 2 + block
        return pltpu.make_async_copy(
            source,
            pairs.at[unit, :, pl.ds(slot * BLOCK, count * BLOCK)],
            pair_sems.at[unit],
        )

    def side_copies(head):
        return [
            pltpu.make_async_copy(sides[i].at[head], side_in.at[head, i], side_sems.at[head, i])
            for i in range(2)
        ]

    for head in range(PER):
        for copy in side_copies(head):
            copy.start()
        for block in range(2):
            side = 1 - block
            from_ext = even if block == 0 else odd
            copy_pair(head, block, at_head(own, head), 0, 2).start()
            pl.when(from_ext)(copy_pair(head, block, at_head(ext, head), 2, 1).start)
            nearby = at_head(arrived[0], head).at[:, pl.ds(side * BLOCK, BLOCK)]
            pl.when(jnp.logical_not(from_ext))(copy_pair(head, block, nearby, 2, 1).start)
            for level in range(LEVELS):
                at = pl.ds(pl.multiple_of(chosen(block, level) * BLOCK, BLOCK), BLOCK)
                source = at_head(arrived[level], head).at[:, at]
                copy_pair(head, block, source, BAND_SLOTS + level, 1).start()

    def out_copies(head):
        copies = [(side_store.at[head, i], side_outs[i].at[head]) for i in range(2)]
        copies.append((acc.at[head, :, pl.ds(0, 2 * BLOCK)], at_head(terms_out, head)))
        copies.append((ext_store.at[head], at_head(ext_out, head)))
        copies += [
            (level_store.at[head, level], at_head(level_outs[level], head).at[:, pl.ds(0, 2 * BLOCK)])
            for level in range(LEVELS)
        ]
        return [
            pltpu.make_async_copy(source, target, out_sems.at[head, i])
            for i, (source, target) in enumerate(copies)
        ]

    def one_head(head, carry):
        acc[head] = jnp.zeros(acc.shape[1:], F32)
        for copy in side_copies(head):
            copy.wait()
        widths = jnp.concatenate(
            [
                side_in[head, i, 1024:1040].astype(F32)[group : group + 1]
                for i in range(2)
                for group in range(2)
            ],
            axis=1,
        )
        width_bias = jnp.where(widths > 1.5, 0.0, NEG)
        for block in range(2):
            unit = head * 2 + block
            side = 1 - block
            outer_valid = device > 0 if block == 0 else device < last
            from_ext = even if block == 0 else odd
            query_t, grad_t = (
                jnp.concatenate(
                    [
                        jnp.transpose(
                            side_in[
                                head,
                                i,
                                (member * 2 + block) * 256 : (member * 2 + block) * 256 + 256,
                            ]
                        )
                        for i in range(2)
                    ],
                    axis=1,
                )
                for member in range(2)
            )
            copy_pair(head, block, at_head(own, head), 0, 2).wait()
            for slot in range(2, SLOTS):
                copy_pair(head, block, at_head(ext, head), slot, 1).wait()
            keys, values = pairs.at[unit, 0], pairs.at[unit, 1]
            outer_bias = width_bias + jnp.where(outer_valid, 0.0, NEG)
            peak = jnp.full((8, ROWS), NEG, F32)
            for slot in range(SLOTS):
                span = slice(slot * BLOCK, slot * BLOCK + BLOCK)
                part = dot(keys[span], query_t, 1, 0)
                if slot == side:
                    part = part + width_bias
                if slot == 2:
                    part = part + outer_bias
                scores[span] = part
                peak = jnp.maximum(peak, jnp.max(part.reshape(BLOCK // 8, 8, ROWS), axis=0))
            peak = jnp.max(peak, axis=0, keepdims=True) * log_scale
            total = jnp.zeros((8, ROWS), F32)
            for slot in range(SLOTS):
                span = slice(slot * BLOCK, slot * BLOCK + BLOCK)
                part = jnp.exp2(scores[span] * log_scale - peak)
                total = total + jnp.sum(part.reshape(BLOCK // 8, 8, ROWS), axis=0)
                exps[span] = part.astype(BF16)
            inverse = 1.0 / jnp.sum(total, axis=0, keepdims=True)
            out_t = (dot(values[...], exps[...], 0, 0) * inverse).astype(BF16)
            grad_t = (grad_t.astype(F32) * inverse).astype(BF16)
            delta = jnp.sum(out_t.astype(F32) * grad_t.astype(F32), axis=0, keepdims=True)
            for slot in range(SLOTS):
                span = slice(slot * BLOCK, slot * BLOCK + BLOCK)
                part = dot(values[span], grad_t, 1, 0)
                dscores[span] = (exps[span].astype(F32) * (part - delta)).astype(BF16)
            dquery_t = (dot(keys[...], dscores[...], 0, 0) * scale).astype(BF16)
            for member, rows_t in enumerate((out_t, dquery_t)):
                first = (member * 2 + block) * 256
                for i in range(2):
                    side_store[head, i, first : first + 256] = jnp.transpose(
                        rows_t[:, i * 256 : i * 256 + 256]
                    )
            outer_row = jnp.where(from_ext, 2, 3 + side)
            for member, (lhs, rhs, factor) in enumerate(
                ((dscores, query_t, scale), (exps, grad_t, None))
            ):
                terms = dot(lhs[...], rhs, 1, 1)
                if factor is not None:
                    terms = terms * factor
                acc[head, member, 0 : 2 * BLOCK] += terms[0 : 2 * BLOCK]
                targets = [outer_row] + [
                    3 + 2 * level + chosen(block, level) for level in range(LEVELS)
                ]
                for slot, row in enumerate(targets):
                    at = pl.ds(pl.multiple_of(row * BLOCK, BLOCK), BLOCK)
                    first = (2 + slot) * BLOCK
                    acc[head, member, at] += terms[first : first + BLOCK]
        for member in range(2):
            ext_store[head, member] = acc[head, member, 2 * BLOCK : 3 * BLOCK].astype(BF16)
            for level in range(LEVELS):
                first = (3 + 2 * level) * BLOCK
                level_store[head, level, member] = acc[
                    head, member, first : first + 2 * BLOCK
                ].astype(BF16)
        for copy in out_copies(head):
            copy.start()
        return carry

    lax.fori_loop(0, PER, one_head, 0)
    for head in range(PER):
        for copy in out_copies(head):
            copy.wait()


def finish_sides_kernel(scalars, *refs):
    sources, targets = refs[:-2], refs[-2:]
    order = query_order(scalars[0], 1)
    for member, target in enumerate(targets):
        for part in range(16):
            block, inner = part // 8, (part % 8) * 16
            pieces = []
            for head in range(2 * LOCAL_HEADS):
                local = head % LOCAL_HEADS
                source = sources[(head // LOCAL_HEADS) * CHUNKS + local // PER]
                for group in range(2):
                    start = (member * 2 + block) * 256 + group * 128 + inner
                    pieces.append(source[local % PER, start : start + 16])
            rows = jnp.concatenate(pieces, axis=0)
            target[part * 256 : part * 256 + 256] = dot(order, rows, 1, 0).astype(BF16)


def finish_pairs_kernel(scalars, *refs):
    even = scalars[0] == 0
    count = (len(refs) - 3) // 2
    far, targets, ins, sems = refs[:count], refs[count : count + 2], refs[count + 2 : -1], refs[-1]
    copies = [
        pltpu.make_async_copy(source, store, sems.at[i])
        for i, (source, store) in enumerate(zip(far, ins))
    ]
    for copy in copies:
        copy.start()
    for copy in copies:
        copy.wait()
    beyond, whole, split = ins[0], ins[1:5], ins[5:]
    order = key_order(1)
    for member, target in enumerate(targets):
        for part in range(4):
            span = slice(part * 64, part * 64 + 64)
            inner = slice((part % 2) * 64, (part % 2) * 64 + 64)
            pieces = []
            for head in range(LOCAL_HEADS):
                total = beyond[head, member, inner].astype(F32)
                total = jnp.where(even if part < 2 else jnp.logical_not(even), total, 0.0)
                for ref in whole:
                    total = total + ref[head, member, span].astype(F32)
                for ref in split[head // PER :: CHUNKS]:
                    total = total + ref[head % PER, member, span].astype(F32)
                pieces.append(total.astype(BF16))
            rows = jnp.concatenate(pieces, axis=0)
            target[part * 256 : part * 256 + 256] = dot(order, rows, 1, 0).astype(BF16)


def flipped(value, mask):
    return lax.ppermute(value, "seq", [(i, i ^ mask) for i in range(lax.axis_size("seq"))])


def past_end(value):
    pairs = []
    for i in range(1, lax.axis_size("seq") - 1, 2):
        pairs += [(i, i + 1), (i + 1, i)]
    return lax.ppermute(value, "seq", pairs)


def other_head(value):
    return lax.ppermute(value, "head", [(0, 1), (1, 0)])


def added(first, second):
    return (first.astype(F32) + second.astype(F32)).astype(BF16)


def shards(query, key_in, value, grad_out, band_width, stride_bits, partner_table):
    rows = key_in.shape[0]
    device = lax.axis_index("seq").astype(jnp.int32)
    place = lax.axis_index("head").astype(jnp.int32)
    odd = device & 1
    match = (stride_bits[None, :] == jnp.arange(LEVELS, dtype=jnp.int32)[:, None]).astype(jnp.int32)
    chosen = jnp.sum(partner_table[:, None, :] * match[None], axis=2)
    scalars = jnp.concatenate(
        [device[None], jnp.full((1,), lax.axis_size("seq") - 1, jnp.int32), chosen.reshape(-1)]
    )

    whole = jax.ShapeDtypeStruct((LOCAL_HEADS, 2, rows, HEAD_DIM), BF16)
    pair = jax.ShapeDtypeStruct((PER, 2, rows, HEAD_DIM), BF16)
    padded = jax.ShapeDtypeStruct((PER, 2, rows + PAD, HEAD_DIM), BF16)
    terms = jax.ShapeDtypeStruct((PER, 2, rows, HEAD_DIM), F32)
    ends = jax.ShapeDtypeStruct((LOCAL_HEADS, 2, BLOCK, HEAD_DIM), BF16)
    sides = jax.ShapeDtypeStruct((PER, 1040, HEAD_DIM), BF16)
    half = jax.ShapeDtypeStruct((PER, 1024, HEAD_DIM), BF16)

    own, own_a, own_b, own_end = pl.pallas_call(
        pack_pairs_kernel,
        out_shape=[whole, padded, padded, ends],
        in_specs=[SCALARS] + [FAR] * 2,
        out_specs=[WHOLE] * 4,
        scratch_shapes=[pltpu.VMEM((rows * 4, HEAD_DIM), BF16)] * 2
        + [pltpu.SemaphoreType.DMA((2, 2))],
        compiler_params=vmem(PACK_MIB),
        name="pack_pairs",
    )(odd[None], key_in.reshape(-1, HEAD_DIM), value.reshape(-1, HEAD_DIM))

    z2_a = flipped(own_a, 32)
    z1 = flipped(own, 16)
    y1 = flipped(own, 2)
    core = flipped(own, 1)
    x = flipped(own, 8)
    keep_a, keep_b, send_a, send_b = pl.pallas_call(
        pack_sides_kernel,
        out_shape=[sides] * (2 * CHUNKS),
        in_specs=[SCALARS] + [FAR] * 3,
        out_specs=[WHOLE] * (2 * CHUNKS),
        scratch_shapes=[pltpu.VMEM((rows * 16, HEAD_DIM), BF16)] * 2
        + [pltpu.SemaphoreType.DMA((2, 4))],
        compiler_params=vmem(SIDES_MIB),
        name="pack_sides",
    )(
        jnp.concatenate([place[None], band_width.reshape(-1)]),
        query.reshape(-1, HEAD_DIM),
        grad_out.reshape(-1, HEAD_DIM),
        core,
    )
    to_z2, to_ext, to_head = lax.optimization_barrier((own_b, own_end, send_a, z1, x, z2_a))[:3]
    z6_a = flipped(z2_a, 96)
    z2_b = flipped(to_z2, 32)
    other_a = other_head(to_head)
    y3 = flipped(y1, 6)
    ext = past_end(to_ext)
    to_head = lax.optimization_barrier((send_b, z2_b, z6_a, other_a, y3, ext))[0]
    z6_b = flipped(z2_b, 96)
    other_b = other_head(to_head)

    def attend(chunk, keep, other, z2, z6, reused):
        ins = [scalars, own, ext, core, y1, y3, x, z1, z2, z6, keep, other, *reused]
        outs = [half, half, terms, ends, *[whole] * 5, padded, padded]
        return pl.pallas_call(
            functools.partial(attend_kernel, chunk * PER, len(reused)),
            out_shape=outs,
            in_specs=[SCALARS] + [FAR] * (len(ins) - 1),
            out_specs=[FAR] * len(outs),
            scratch_shapes=[
                pltpu.VMEM((SLOTS * BLOCK, ROWS), F32),
                pltpu.VMEM((SLOTS * BLOCK, ROWS), BF16),
                pltpu.VMEM((SLOTS * BLOCK, ROWS), BF16),
                pltpu.VMEM((2 * PER, 2, SLOTS * BLOCK, HEAD_DIM), BF16),
                pltpu.VMEM((PER, 2, 1040, HEAD_DIM), BF16),
                pltpu.VMEM((PER, 2, 1024, HEAD_DIM), BF16),
                pltpu.VMEM((PER, 2, (3 + 2 * LEVELS) * BLOCK, HEAD_DIM), F32),
                pltpu.VMEM((PER, 2, BLOCK, HEAD_DIM), BF16),
                pltpu.VMEM((PER, LEVELS, 2, rows, HEAD_DIM), BF16),
                pltpu.SemaphoreType.DMA((2 * PER,)),
                pltpu.SemaphoreType.DMA((PER, 2)),
                pltpu.SemaphoreType.DMA((PER, 4 + LEVELS)),
            ],
            input_output_aliases={12 + i: 3 + i for i in range(len(reused))},
            compiler_params=vmem(18),
            cost_estimate=pl.CostEstimate(
                flops=PER * 2 * 12 * SLOTS * BLOCK * ROWS * HEAD_DIM,
                transcendentals=PER * 2 * SLOTS * BLOCK * ROWS,
                bytes_accessed=PER * 24 * rows * HEAD_DIM * 4,
            ),
            name="attend",
        )(*ins)

    first = attend(0, keep_a, other_a, z2_a, z6_a, [])
    keep_out_a, other_out_a, terms_a = first[:3]
    z2_terms_a, z4_terms_a = first[9:]
    far_a = flipped(z4_terms_a, 96)
    swapped_a = other_head(other_out_a)
    second = attend(1, keep_b, other_b, z2_b, z6_b, first[3:9])
    keep_out_b, other_out_b, terms_b, ext_terms, core_terms, y1_terms, y2_terms = second[:7]
    x_terms, z1_terms, z2_terms_b, z4_terms_b = second[7:]
    to_z6, to_y3, to_x, to_ext, far_a, swapped_a = lax.optimization_barrier(
        (z4_terms_b, y2_terms, x_terms, ext_terms, far_a, swapped_a)
    )
    far_b = flipped(to_z6, 96)
    back_z2_a = flipped(added(z2_terms_a, far_a), 32)
    near = flipped(to_y3, 6)
    back_x = flipped(to_x, 8)
    back_ext = past_end(to_ext)
    far_b, back_z2_a, near, back_x, back_ext, z1_terms, core_terms, other_out_b = (
        lax.optimization_barrier(
            (far_b, back_z2_a, near, back_x, back_ext, z1_terms, core_terms, other_out_b)
        )
    )
    back_z2_b = flipped(added(z2_terms_b, far_b), 32)
    back_y = flipped(added(y1_terms, near), 2)
    swapped_b = other_head(other_out_b)
    back_z1 = flipped(z1_terms, 16)
    back_core = flipped(core_terms, 1)

    out, dquery = pl.pallas_call(
        finish_sides_kernel,
        out_shape=[jax.ShapeDtypeStruct((rows * 16, HEAD_DIM), BF16)] * 2,
        in_specs=[SCALARS] + [WHOLE] * (2 * CHUNKS),
        out_specs=[WHOLE] * 2,
        compiler_params=vmem(8),
        name="finish_sides",
    )(place[None], keep_out_a, keep_out_b, swapped_a, swapped_b)
    sums = [back_ext, back_core, back_y, back_x, back_z1]
    sums += [terms_a, terms_b, back_z2_a, back_z2_b]
    dkey, dvalue = pl.pallas_call(
        finish_pairs_kernel,
        out_shape=[jax.ShapeDtypeStruct((rows * 4, HEAD_DIM), BF16)] * 2,
        in_specs=[SCALARS] + [FAR] * len(sums),
        out_specs=[WHOLE] * 2,
        scratch_shapes=[pltpu.VMEM(part.shape, part.dtype) for part in sums]
        + [pltpu.SemaphoreType.DMA((len(sums),))],
        compiler_params=vmem(16),
        name="finish_pairs",
    )(odd[None], *sums)
    return (
        out.reshape(query.shape),
        dquery.reshape(query.shape),
        dkey.reshape(key_in.shape),
        dvalue.reshape(key_in.shape),
    )


def solution(mesh):
    placed = (
        P("seq", None, "head", None),
        P("seq", "head", None),
        P("seq", "head", None),
        P("seq", None, "head", None),
        P(None, "head"),
        P(),
        P("seq", None),
    )
    return jax.shard_map(
        shards,
        mesh=mesh,
        in_specs=placed,
        out_specs=(
            P("seq", None, "head", None),
            P("seq", None, "head", None),
            P("seq", "head", None),
            P("seq", "head", None),
        ),
        check_vma=False,
    )
```

```python
import functools
import math

import jax
import jax.numpy as jnp
from jax import lax
from jax.experimental import pallas as pl
from jax.experimental.pallas import tpu as pltpu
from jax.sharding import PartitionSpec as P

BLOCK = 128
HEAD_DIM = 128
CHUNKS = 2
LOCAL_HEADS = 4
PER = LOCAL_HEADS // CHUNKS
LEVELS = 7
BAND_SLOTS = 3
SLOTS = BAND_SLOTS + LEVELS
ROWS = 512
PAD = 8
PACK_MIB = 56
SIDES_MIB = 8
ATT_MIB = 18
NEG = -1e30
F32 = jnp.float32
BF16 = jnp.bfloat16
WHOLE = pl.BlockSpec(memory_space=pltpu.VMEM)
FAR = pl.BlockSpec(memory_space=pltpu.HBM)
SCALARS = pl.BlockSpec(memory_space=pltpu.SMEM)


def vmem(mib):
    return pltpu.CompilerParams(vmem_limit_bytes=mib << 20)


def dot(lhs, rhs, lhs_dim, rhs_dim):
    return lax.dot_general(
        lhs, rhs, (((lhs_dim,), (rhs_dim,)), ((), ())), preferred_element_type=F32
    )


def query_order(place, rows_first):
    ordered = lax.broadcasted_iota(jnp.int32, (256, 256), rows_first)
    natural = lax.broadcasted_iota(jnp.int32, (256, 256), 1 - rows_first)
    source = (ordered & 15) * 16 + ((ordered >> 4) ^ (place * 8))
    return (natural == source).astype(BF16)


def key_order(rows_first):
    ordered = lax.broadcasted_iota(jnp.int32, (256, 256), rows_first)
    natural = lax.broadcasted_iota(jnp.int32, (256, 256), 1 - rows_first)
    return (natural == (ordered & 63) * 4 + (ordered >> 6)).astype(BF16)


def pieces_of(ref, store, sems, count):
    rows = ref.shape[0] // count
    copies = [
        pltpu.make_async_copy(
            ref.at[pl.ds(i * rows, rows)], store.at[pl.ds(i * rows, rows)], sems.at[i]
        )
        for i in range(count)
    ]
    for copy in copies:
        copy.start()
    return copies


def pack_pairs_kernel(scalars, key, value, *refs):
    whole, first, second, ends, key_in, value_in, sems = refs
    even = scalars[0] == 0
    copies = [
        pieces_of(ref, store, sems.at[member], 2)
        for member, (ref, store) in enumerate(((key, key_in), (value, value_in)))
    ]
    order = key_order(0)
    for block in range(2):
        for member, store in enumerate((key_in, value_in)):
            copies[member][block].wait()
            for inner in (0, 64):
                start = block * 512 + inner * 4
                rows = dot(order, store[start : start + 256], 1, 0).astype(BF16)
                span = slice(block * BLOCK + inner, block * BLOCK + inner + 64)
                end = slice(inner, inner + 64)
                for head in range(LOCAL_HEADS):
                    piece = rows[head * 64 : head * 64 + 64]
                    whole[head, member, span] = piece
                    (first, second)[head // PER][head % PER, member, span] = piece
                    if block == 0:
                        ends[head, member, end] = piece
                    else:
                        ends[head, member, end] = jnp.where(even, ends[head, member, end], piece)


def pack_sides_kernel(scalars, query, grad, unused, *refs):
    place = scalars[0]
    keeps, sends = refs[:CHUNKS], refs[CHUNKS : 2 * CHUNKS]
    stores, sems = refs[2 * CHUNKS : 2 * CHUNKS + 2], refs[2 * CHUNKS + 2]
    copies = [
        pieces_of(ref, store, sems.at[member], 4)
        for member, (ref, store) in enumerate(zip((query, grad), stores))
    ]
    order = query_order(place, 0)
    for part in range(16):
        for member, store in enumerate(stores):
            if part % 4 == 0:
                copies[member][part // 4].wait()
            rows = dot(order, store[part * 256 : part * 256 + 256], 1, 0).astype(BF16)
            block, inner = part // 8, (part % 8) * 16
            for head in range(2 * LOCAL_HEADS):
                target = (keeps, sends)[head // LOCAL_HEADS]
                local = head % LOCAL_HEADS
                for group in range(2):
                    start = (member * 2 + block) * 256 + group * 128 + inner
                    first = (head * 2 + group) * 16
                    target[local // PER][local % PER, start : start + 16] = rows[first : first + 16]
    sublane = lax.broadcasted_iota(jnp.int32, (16, HEAD_DIM), 0)
    for head in range(2 * LOCAL_HEADS):
        target = (keeps, sends)[head // LOCAL_HEADS]
        local = head % LOCAL_HEADS
        actual = head ^ (place * LOCAL_HEADS)
        width = jnp.where(sublane == 0, scalars[1 + actual * 2], scalars[2 + actual * 2])
        target[local // PER][local % PER, 1024:1040] = width.astype(F32).astype(BF16)


def attend_kernel(base, reused, scalars, *refs):
    own, ext = refs[:2]
    arrived = refs[2 : 2 + LEVELS]
    sides = refs[2 + LEVELS : 4 + LEVELS]
    refs = refs[4 + LEVELS + reused :]
    side_outs, terms_out, ext_out = refs[:2], refs[2], refs[3]
    level_outs = refs[4 : 4 + LEVELS]
    (scores, exps, dscores, pairs, side_in, side_store, acc, ext_store, level_store) = refs[
        4 + LEVELS : 13 + LEVELS
    ]
    pair_sems, side_sems, out_sems = refs[13 + LEVELS :]
    device = scalars[0]
    last = scalars[1]
    even = (device & 1) == 0
    odd = jnp.logical_not(even)
    scale = HEAD_DIM**-0.5
    log_scale = scale * math.log2(math.e)

    def chosen(block, level):
        return scalars[2 + block * LEVELS + level]

    def at_head(ref, head):
        return ref.at[head + base if ref.shape[0] == LOCAL_HEADS else head]

    def copy_pair(head, block, source, slot, count):
        unit = head * 2 + block
        return pltpu.make_async_copy(
            source,
            pairs.at[unit, :, pl.ds(slot * BLOCK, count * BLOCK)],
            pair_sems.at[unit],
        )

    def side_copies(head):
        return [
            pltpu.make_async_copy(sides[i].at[head], side_in.at[head, i], side_sems.at[head, i])
            for i in range(2)
        ]

    for head in range(PER):
        for copy in side_copies(head):
            copy.start()
        for block in range(2):
            side = 1 - block
            from_ext = even if block == 0 else odd
            copy_pair(head, block, at_head(own, head), 0, 2).start()
            pl.when(from_ext)(copy_pair(head, block, at_head(ext, head), 2, 1).start)
            nearby = at_head(arrived[0], head).at[:, pl.ds(side * BLOCK, BLOCK)]
            pl.when(jnp.logical_not(from_ext))(copy_pair(head, block, nearby, 2, 1).start)
            for level in range(LEVELS):
                at = pl.ds(pl.multiple_of(chosen(block, level) * BLOCK, BLOCK), BLOCK)
                source = at_head(arrived[level], head).at[:, at]
                copy_pair(head, block, source, BAND_SLOTS + level, 1).start()

    def out_copies(head):
        copies = [(side_store.at[head, i], side_outs[i].at[head]) for i in range(2)]
        copies.append((acc.at[head, :, pl.ds(0, 2 * BLOCK)], at_head(terms_out, head)))
        copies.append((ext_store.at[head], at_head(ext_out, head)))
        copies += [
            (level_store.at[head, level], at_head(level_outs[level], head).at[:, pl.ds(0, 2 * BLOCK)])
            for level in range(LEVELS)
        ]
        return [
            pltpu.make_async_copy(source, target, out_sems.at[head, i])
            for i, (source, target) in enumerate(copies)
        ]

    def one_head(head, carry):
        acc[head] = jnp.zeros(acc.shape[1:], F32)
        for copy in side_copies(head):
            copy.wait()
        widths = jnp.concatenate(
            [
                side_in[head, i, 1024:1040].astype(F32)[group : group + 1]
                for i in range(2)
                for group in range(2)
            ],
            axis=1,
        )
        width_bias = jnp.where(widths > 1.5, 0.0, NEG)
        for block in range(2):
            unit = head * 2 + block
            side = 1 - block
            outer_valid = device > 0 if block == 0 else device < last
            from_ext = even if block == 0 else odd
            query_t, grad_t = (
                jnp.concatenate(
                    [
                        jnp.transpose(
                            side_in[
                                head,
                                i,
                                (member * 2 + block) * 256 : (member * 2 + block) * 256 + 256,
                            ]
                        )
                        for i in range(2)
                    ],
                    axis=1,
                )
                for member in range(2)
            )
            copy_pair(head, block, at_head(own, head), 0, 2).wait()
            for slot in range(2, SLOTS):
                copy_pair(head, block, at_head(ext, head), slot, 1).wait()
            keys, values = pairs.at[unit, 0], pairs.at[unit, 1]
            outer_bias = width_bias + jnp.where(outer_valid, 0.0, NEG)
            peak = jnp.full((8, ROWS), NEG, F32)
            for slot in range(SLOTS):
                span = slice(slot * BLOCK, slot * BLOCK + BLOCK)
                part = dot(keys[span], query_t, 1, 0)
                if slot == side:
                    part = part + width_bias
                if slot == 2:
                    part = part + outer_bias
                scores[span] = part
                peak = jnp.maximum(peak, jnp.max(part.reshape(BLOCK // 8, 8, ROWS), axis=0))
            peak = jnp.max(peak, axis=0, keepdims=True) * log_scale
            total = jnp.zeros((8, ROWS), F32)
            for slot in range(SLOTS):
                span = slice(slot * BLOCK, slot * BLOCK + BLOCK)
                part = jnp.exp2(scores[span] * log_scale - peak)
                total = total + jnp.sum(part.reshape(BLOCK // 8, 8, ROWS), axis=0)
                exps[span] = part.astype(BF16)
            inverse = 1.0 / jnp.sum(total, axis=0, keepdims=True)
            out_t = (dot(values[...], exps[...], 0, 0) * inverse).astype(BF16)
            grad_t = (grad_t.astype(F32) * inverse).astype(BF16)
            delta = jnp.sum(out_t.astype(F32) * grad_t.astype(F32), axis=0, keepdims=True)
            for slot in range(SLOTS):
                span = slice(slot * BLOCK, slot * BLOCK + BLOCK)
                part = dot(values[span], grad_t, 1, 0)
                dscores[span] = (exps[span].astype(F32) * (part - delta)).astype(BF16)
            dquery_t = (dot(keys[...], dscores[...], 0, 0) * scale).astype(BF16)
            for member, rows_t in enumerate((out_t, dquery_t)):
                first = (member * 2 + block) * 256
                for i in range(2):
                    side_store[head, i, first : first + 256] = jnp.transpose(
                        rows_t[:, i * 256 : i * 256 + 256]
                    )
            outer_row = jnp.where(from_ext, 2, 3 + side)
            for member, (lhs, rhs, factor) in enumerate(
                ((dscores, query_t, scale), (exps, grad_t, None))
            ):
                terms = dot(lhs[...], rhs, 1, 1)
                if factor is not None:
                    terms = terms * factor
                acc[head, member, 0 : 2 * BLOCK] += terms[0 : 2 * BLOCK]
                targets = [outer_row] + [
                    3 + 2 * level + chosen(block, level) for level in range(LEVELS)
                ]
                for slot, row in enumerate(targets):
                    at = pl.ds(pl.multiple_of(row * BLOCK, BLOCK), BLOCK)
                    first = (2 + slot) * BLOCK
                    acc[head, member, at] += terms[first : first + BLOCK]
        for member in range(2):
            ext_store[head, member] = acc[head, member, 2 * BLOCK : 3 * BLOCK].astype(BF16)
            for level in range(LEVELS):
                first = (3 + 2 * level) * BLOCK
                level_store[head, level, member] = acc[
                    head, member, first : first + 2 * BLOCK
                ].astype(BF16)
        for copy in out_copies(head):
            copy.start()
        return carry

    lax.fori_loop(0, PER, one_head, 0)
    for head in range(PER):
        for copy in out_copies(head):
            copy.wait()


def attend_scratch(rows):
    return [
        pltpu.VMEM((SLOTS * BLOCK, ROWS), F32),
        pltpu.VMEM((SLOTS * BLOCK, ROWS), BF16),
        pltpu.VMEM((SLOTS * BLOCK, ROWS), BF16),
        pltpu.VMEM((2 * PER, 2, SLOTS * BLOCK, HEAD_DIM), BF16),
        pltpu.VMEM((PER, 2, 1040, HEAD_DIM), BF16),
        pltpu.VMEM((PER, 2, 1024, HEAD_DIM), BF16),
        pltpu.VMEM((PER, 2, (3 + 2 * LEVELS) * BLOCK, HEAD_DIM), F32),
        pltpu.VMEM((PER, 2, BLOCK, HEAD_DIM), BF16),
        pltpu.VMEM((PER, LEVELS, 2, rows, HEAD_DIM), BF16),
        pltpu.SemaphoreType.DMA((2 * PER,)),
        pltpu.SemaphoreType.DMA((PER, 2)),
        pltpu.SemaphoreType.DMA((PER, 4 + LEVELS)),
    ]


def finish_sides_kernel(scalars, *refs):
    sources, targets = refs[:-2], refs[-2:]
    order = query_order(scalars[0], 1)
    for member, target in enumerate(targets):
        for part in range(16):
            block, inner = part // 8, (part % 8) * 16
            pieces = []
            for head in range(2 * LOCAL_HEADS):
                local = head % LOCAL_HEADS
                source = sources[(head // LOCAL_HEADS) * CHUNKS + local // PER]
                for group in range(2):
                    start = (member * 2 + block) * 256 + group * 128 + inner
                    pieces.append(source[local % PER, start : start + 16])
            rows = jnp.concatenate(pieces, axis=0)
            target[part * 256 : part * 256 + 256] = dot(order, rows, 1, 0).astype(BF16)


def finish_pairs_kernel(scalars, *refs):
    even = scalars[0] == 0
    count = (len(refs) - 3) // 2
    far, targets, ins, sems = refs[:count], refs[count : count + 2], refs[count + 2 : -1], refs[-1]
    copies = [
        pltpu.make_async_copy(source, store, sems.at[i])
        for i, (source, store) in enumerate(zip(far, ins))
    ]
    for copy in copies:
        copy.start()
    for copy in copies:
        copy.wait()
    beyond, whole, split = ins[0], ins[1:4], ins[4:]
    order = key_order(1)
    for member, target in enumerate(targets):
        for part in range(4):
            span = slice(part * 64, part * 64 + 64)
            inner = slice((part % 2) * 64, (part % 2) * 64 + 64)
            pieces = []
            for head in range(LOCAL_HEADS):
                total = beyond[head, member, inner].astype(F32)
                total = jnp.where(even if part < 2 else jnp.logical_not(even), total, 0.0)
                for ref in whole:
                    total = total + ref[head, member, span].astype(F32)
                for ref in split[head // PER :: CHUNKS]:
                    total = total + ref[head % PER, member, span].astype(F32)
                pieces.append(total.astype(BF16))
            rows = jnp.concatenate(pieces, axis=0)
            target[part * 256 : part * 256 + 256] = dot(order, rows, 1, 0).astype(BF16)


def flipped(value, mask):
    return lax.ppermute(value, "seq", [(i, i ^ mask) for i in range(lax.axis_size("seq"))])


def past_end(value):
    pairs = []
    for i in range(1, lax.axis_size("seq") - 1, 2):
        pairs += [(i, i + 1), (i + 1, i)]
    return lax.ppermute(value, "seq", pairs)


def other_head(value):
    return lax.ppermute(value, "head", [(0, 1), (1, 0)])


def added(first, second):
    return (first.astype(F32) + second.astype(F32)).astype(BF16)


def shards(query, key_in, value, grad_out, band_width, stride_bits, partner_table):
    rows = key_in.shape[0]
    device = lax.axis_index("seq").astype(jnp.int32)
    place = lax.axis_index("head").astype(jnp.int32)
    odd = device & 1
    match = (stride_bits[None, :] == jnp.arange(LEVELS, dtype=jnp.int32)[:, None]).astype(jnp.int32)
    chosen = jnp.sum(partner_table[:, None, :] * match[None], axis=2)
    scalars = jnp.concatenate(
        [device[None], jnp.full((1,), lax.axis_size("seq") - 1, jnp.int32), chosen.reshape(-1)]
    )

    whole = jax.ShapeDtypeStruct((LOCAL_HEADS, 2, rows, HEAD_DIM), BF16)
    pair = jax.ShapeDtypeStruct((PER, 2, rows, HEAD_DIM), BF16)
    padded = jax.ShapeDtypeStruct((PER, 2, rows + PAD, HEAD_DIM), BF16)
    terms = jax.ShapeDtypeStruct((PER, 2, rows, HEAD_DIM), F32)
    ends = jax.ShapeDtypeStruct((LOCAL_HEADS, 2, BLOCK, HEAD_DIM), BF16)
    sides = jax.ShapeDtypeStruct((PER, 1040, HEAD_DIM), BF16)
    half = jax.ShapeDtypeStruct((PER, 1024, HEAD_DIM), BF16)

    own, own_a, own_b, own_end = pl.pallas_call(
        pack_pairs_kernel,
        out_shape=[whole, padded, padded, ends],
        in_specs=[SCALARS] + [FAR] * 2,
        out_specs=[WHOLE] * 4,
        scratch_shapes=[pltpu.VMEM((rows * 4, HEAD_DIM), BF16)] * 2
        + [pltpu.SemaphoreType.DMA((2, 2))],
        compiler_params=vmem(PACK_MIB),
        name="pack_pairs",
    )(odd[None], key_in.reshape(-1, HEAD_DIM), value.reshape(-1, HEAD_DIM))

    z2_a = flipped(own_a, 32)
    z1_a = flipped(own_a, 16)
    y1 = flipped(own, 2)
    core = flipped(own, 1)
    x = flipped(own, 8)
    ext = past_end(lax.optimization_barrier((own_end, core))[0])
    keep_a, keep_b, send_a, send_b = pl.pallas_call(
        pack_sides_kernel,
        out_shape=[sides] * (2 * CHUNKS),
        in_specs=[SCALARS] + [FAR] * 3,
        out_specs=[WHOLE] * (2 * CHUNKS),
        scratch_shapes=[pltpu.VMEM((rows * 16, HEAD_DIM), BF16)] * 2
        + [pltpu.SemaphoreType.DMA((2, 4))],
        compiler_params=vmem(SIDES_MIB),
        name="pack_sides",
    )(
        jnp.concatenate([place[None], band_width.reshape(-1)]),
        query.reshape(-1, HEAD_DIM),
        grad_out.reshape(-1, HEAD_DIM),
        core,
    )
    to_z2, to_head = lax.optimization_barrier((own_b, send_a))
    z6_a = flipped(z2_a, 96)
    z2_b = flipped(to_z2, 32)
    other_a = other_head(to_head)
    y3 = flipped(y1, 6)
    to_head, to_z1 = lax.optimization_barrier((send_b, to_z2))
    z6_b = flipped(z2_b, 96)
    z1_b = flipped(to_z1, 16)
    other_b = other_head(to_head)

    def attend(chunk, keep, other, z1, z2, z6, reused):
        ins = [scalars, own, ext, core, y1, y3, x, z1, z2, z6, keep, other, *reused]
        outs = [half, half, terms, ends, *[whole] * 4, padded, padded, padded]
        return pl.pallas_call(
            functools.partial(attend_kernel, chunk * PER, len(reused)),
            out_shape=outs,
            in_specs=[SCALARS] + [FAR] * (len(ins) - 1),
            out_specs=[FAR] * len(outs),
            scratch_shapes=attend_scratch(rows),
            input_output_aliases={12 + i: 3 + i for i in range(len(reused))},
            compiler_params=vmem(ATT_MIB),
            cost_estimate=pl.CostEstimate(
                flops=PER * 2 * 12 * SLOTS * BLOCK * ROWS * HEAD_DIM,
                transcendentals=PER * 2 * SLOTS * BLOCK * ROWS,
                bytes_accessed=PER * 24 * rows * HEAD_DIM * 4,
            ),
            name="attend",
        )(*ins)

    first = attend(0, keep_a, other_a, z1_a, z2_a, z6_a, [])
    keep_out_a, other_out_a, terms_a = first[:3]
    z1_terms_a, z2_terms_a, z4_terms_a = first[8:]
    far_a = flipped(z4_terms_a, 96)
    swapped_a = other_head(other_out_a)
    back_z1_a = flipped(z1_terms_a, 16)
    second = attend(1, keep_b, other_b, z1_b, z2_b, z6_b, first[3:8])
    keep_out_b, other_out_b, terms_b, ext_terms, core_terms, y1_terms, y2_terms = second[:7]
    x_terms, z1_terms_b, z2_terms_b, z4_terms_b = second[7:]
    to_z6, to_y3, to_x, to_ext, far_a, swapped_a, back_z1_a = lax.optimization_barrier(
        (z4_terms_b, y2_terms, x_terms, ext_terms, far_a, swapped_a, back_z1_a)
    )
    far_b = flipped(to_z6, 96)
    back_z2_a = flipped(added(z2_terms_a, far_a), 32)
    near = flipped(to_y3, 6)
    back_x = flipped(to_x, 8)
    back_ext = past_end(to_ext)
    far_b, back_z2_a, near, back_x, back_ext, z1_terms_b, core_terms, other_out_b = (
        lax.optimization_barrier(
            (far_b, back_z2_a, near, back_x, back_ext, z1_terms_b, core_terms, other_out_b)
        )
    )
    back_z2_b = flipped(added(z2_terms_b, far_b), 32)
    back_y = flipped(added(y1_terms, near), 2)
    swapped_b = other_head(other_out_b)
    back_z1_b = flipped(z1_terms_b, 16)
    back_core = flipped(core_terms, 1)

    out, dquery = pl.pallas_call(
        finish_sides_kernel,
        out_shape=[jax.ShapeDtypeStruct((rows * 16, HEAD_DIM), BF16)] * 2,
        in_specs=[SCALARS] + [WHOLE] * (2 * CHUNKS),
        out_specs=[WHOLE] * 2,
        compiler_params=vmem(8),
        name="finish_sides",
    )(place[None], keep_out_a, keep_out_b, swapped_a, swapped_b)
    sums = [back_ext, back_core, back_y, back_x, terms_a, terms_b]
    sums += [back_z1_a, back_z1_b, back_z2_a, back_z2_b]
    dkey, dvalue = pl.pallas_call(
        finish_pairs_kernel,
        out_shape=[jax.ShapeDtypeStruct((rows * 4, HEAD_DIM), BF16)] * 2,
        in_specs=[SCALARS] + [FAR] * len(sums),
        out_specs=[WHOLE] * 2,
        scratch_shapes=[pltpu.VMEM(part.shape, part.dtype) for part in sums]
        + [pltpu.SemaphoreType.DMA((len(sums),))],
        compiler_params=vmem(16),
        name="finish_pairs",
    )(odd[None], *sums)
    return (
        out.reshape(query.shape),
        dquery.reshape(query.shape),
        dkey.reshape(key_in.shape),
        dvalue.reshape(key_in.shape),
    )


def solution(mesh):
    placed = (
        P("seq", None, "head", None),
        P("seq", "head", None),
        P("seq", "head", None),
        P("seq", None, "head", None),
        P(None, "head"),
        P(),
        P("seq", None),
    )
    return jax.shard_map(
        shards,
        mesh=mesh,
        in_specs=placed,
        out_specs=(
            P("seq", None, "head", None),
            P("seq", None, "head", None),
            P("seq", "head", None),
            P("seq", "head", None),
        ),
        check_vma=False,
    )
```

```python
import functools
import math

import jax
import jax.numpy as jnp
from jax import lax
from jax.experimental import pallas as pl
from jax.experimental.pallas import tpu as pltpu
from jax.sharding import PartitionSpec as P

BLOCK = 128
HEAD_DIM = 128
CHUNKS = 2
LOCAL_HEADS = 4
PER = LOCAL_HEADS // CHUNKS
LEVELS = 7
BAND_SLOTS = 3
SLOTS = BAND_SLOTS + LEVELS
ROWS = 512
PAD = 8
PACK_MIB = 56
SIDES_MIB = 8
ATT_MIB = 24
NEG = -1e30
F32 = jnp.float32
BF16 = jnp.bfloat16
WHOLE = pl.BlockSpec(memory_space=pltpu.VMEM)
FAR = pl.BlockSpec(memory_space=pltpu.HBM)
SCALARS = pl.BlockSpec(memory_space=pltpu.SMEM)


def vmem(mib):
    return pltpu.CompilerParams(vmem_limit_bytes=mib << 20)


def dot(lhs, rhs, lhs_dim, rhs_dim):
    return lax.dot_general(
        lhs, rhs, (((lhs_dim,), (rhs_dim,)), ((), ())), preferred_element_type=F32
    )


def query_order(place, rows_first):
    ordered = lax.broadcasted_iota(jnp.int32, (256, 256), rows_first)
    natural = lax.broadcasted_iota(jnp.int32, (256, 256), 1 - rows_first)
    source = (ordered & 15) * 16 + ((ordered >> 4) ^ (place * 8))
    return (natural == source).astype(BF16)


def key_order(rows_first):
    ordered = lax.broadcasted_iota(jnp.int32, (256, 256), rows_first)
    natural = lax.broadcasted_iota(jnp.int32, (256, 256), 1 - rows_first)
    return (natural == (ordered & 63) * 4 + (ordered >> 6)).astype(BF16)


def pieces_of(ref, store, sems, count):
    rows = ref.shape[0] // count
    copies = [
        pltpu.make_async_copy(
            ref.at[pl.ds(i * rows, rows)], store.at[pl.ds(i * rows, rows)], sems.at[i]
        )
        for i in range(count)
    ]
    for copy in copies:
        copy.start()
    return copies


def pack_pairs_kernel(scalars, key, value, *refs):
    whole, first, second, ends, key_in, value_in, sems = refs
    even = scalars[0] == 0
    copies = [
        pieces_of(ref, store, sems.at[member], 2)
        for member, (ref, store) in enumerate(((key, key_in), (value, value_in)))
    ]
    order = key_order(0)
    for block in range(2):
        for member, store in enumerate((key_in, value_in)):
            copies[member][block].wait()
            for inner in (0, 64):
                start = block * 512 + inner * 4
                rows = dot(order, store[start : start + 256], 1, 0).astype(BF16)
                span = slice(block * BLOCK + inner, block * BLOCK + inner + 64)
                end = slice(inner, inner + 64)
                for head in range(LOCAL_HEADS):
                    piece = rows[head * 64 : head * 64 + 64]
                    whole[head, member, span] = piece
                    (first, second)[head // PER][head % PER, member, span] = piece
                    if block == 0:
                        ends[head, member, end] = piece
                    else:
                        ends[head, member, end] = jnp.where(even, ends[head, member, end], piece)


def pack_sides_kernel(scalars, query, grad, unused, *refs):
    place = scalars[0]
    keeps, sends = refs[:CHUNKS], refs[CHUNKS : 2 * CHUNKS]
    stores, sems = refs[2 * CHUNKS : 2 * CHUNKS + 2], refs[2 * CHUNKS + 2]
    copies = [
        pieces_of(ref, store, sems.at[member], 4)
        for member, (ref, store) in enumerate(zip((query, grad), stores))
    ]
    order = query_order(place, 0)
    for part in range(16):
        for member, store in enumerate(stores):
            if part % 4 == 0:
                copies[member][part // 4].wait()
            rows = dot(order, store[part * 256 : part * 256 + 256], 1, 0).astype(BF16)
            block, inner = part // 8, (part % 8) * 16
            for head in range(2 * LOCAL_HEADS):
                target = (keeps, sends)[head // LOCAL_HEADS]
                local = head % LOCAL_HEADS
                for group in range(2):
                    start = (member * 2 + block) * 256 + group * 128 + inner
                    first = (head * 2 + group) * 16
                    target[local // PER][local % PER, start : start + 16] = rows[first : first + 16]
    sublane = lax.broadcasted_iota(jnp.int32, (16, HEAD_DIM), 0)
    for head in range(2 * LOCAL_HEADS):
        target = (keeps, sends)[head // LOCAL_HEADS]
        local = head % LOCAL_HEADS
        actual = head ^ (place * LOCAL_HEADS)
        width = jnp.where(sublane == 0, scalars[1 + actual * 2], scalars[2 + actual * 2])
        target[local // PER][local % PER, 1024:1040] = width.astype(F32).astype(BF16)


def attend_kernel(base, reused, scalars, *refs):
    own, ext = refs[:2]
    arrived = refs[2 : 2 + LEVELS]
    sides = refs[2 + LEVELS : 4 + LEVELS]
    refs = refs[4 + LEVELS + reused :]
    side_outs, terms_out, ext_out = refs[:2], refs[2], refs[3]
    level_outs = refs[4 : 4 + LEVELS]
    (scores, exps, dscores, pairs, side_in, side_store, acc, ext_store, level_store) = refs[
        4 + LEVELS : 13 + LEVELS
    ]
    pair_sems, side_sems, out_sems = refs[13 + LEVELS :]
    device = scalars[0]
    last = scalars[1]
    even = (device & 1) == 0
    odd = jnp.logical_not(even)
    scale = HEAD_DIM**-0.5
    log_scale = scale * math.log2(math.e)

    def chosen(block, level):
        return scalars[2 + block * LEVELS + level]

    def at_head(ref, head):
        return ref.at[head + base if ref.shape[0] == LOCAL_HEADS else head]

    def copy_pair(head, block, source, slot, count):
        unit = head * 2 + block
        return pltpu.make_async_copy(
            source,
            pairs.at[unit, :, pl.ds(slot * BLOCK, count * BLOCK)],
            pair_sems.at[unit],
        )

    def side_copies(head):
        return [
            pltpu.make_async_copy(sides[i].at[head], side_in.at[head, i], side_sems.at[head, i])
            for i in range(2)
        ]

    def start_unit(unit):
        head, block = unit // 2, unit % 2
        side = 1 - block
        from_ext = even if block == 0 else odd
        copy_pair(head, block, at_head(own, head).at[:, pl.ds(0, 2 * BLOCK)], 0, 2).start()
        pl.when(from_ext)(copy_pair(head, block, at_head(ext, head), 2, 1).start)
        nearby = at_head(arrived[0], head).at[:, pl.ds(side * BLOCK, BLOCK)]
        pl.when(jnp.logical_not(from_ext))(copy_pair(head, block, nearby, 2, 1).start)
        for level in range(LEVELS):
            at = pl.ds(pl.multiple_of(chosen(block, level) * BLOCK, BLOCK), BLOCK)
            source = at_head(arrived[level], head).at[:, at]
            copy_pair(head, block, source, BAND_SLOTS + level, 1).start()

    def wait_unit(unit):
        head, block = unit // 2, unit % 2
        copy_pair(head, block, at_head(own, head).at[:, pl.ds(0, 2 * BLOCK)], 0, 2).wait()
        for slot in range(2, SLOTS):
            copy_pair(head, block, at_head(ext, head), slot, 1).wait()

    def side_out(head, i):
        return pltpu.make_async_copy(
            side_store.at[head, i], side_outs[i].at[head], out_sems.at[head, 2, i]
        )

    def term_copies(head, member):
        copies = [
            (acc.at[head, member, pl.ds(0, 2 * BLOCK)], at_head(terms_out, head).at[member]),
            (ext_store.at[head, member], at_head(ext_out, head).at[member]),
        ]
        copies += [
            (
                level_store.at[head, level, member],
                at_head(level_outs[level], head).at[member, pl.ds(0, 2 * BLOCK)],
            )
            for level in range(LEVELS)
        ]
        return [
            pltpu.make_async_copy(source, target, out_sems.at[head, member, i])
            for i, (source, target) in enumerate(copies)
        ]

    def unit_stages(unit):
        head, block = unit // 2, unit % 2
        side = 1 - block
        state = {}
        keys, values = pairs.at[unit, 0], pairs.at[unit, 1]
        score, weight, dscore = (ref.at[unit % 2] for ref in (scores, exps, dscores))

        def span_of(slot, count=1):
            return slice(slot * BLOCK, (slot + count) * BLOCK)

        def score_stage():
            if block == 0:
                for copy in side_copies(head):
                    copy.wait()
            widths = jnp.concatenate(
                [
                    side_in[head, i, 1024:1040].astype(F32)[group : group + 1]
                    for i in range(2)
                    for group in range(2)
                ],
                axis=1,
            )
            width_bias = jnp.where(widths > 1.5, 0.0, NEG)
            outer_valid = device > 0 if block == 0 else device < last
            outer_bias = width_bias + jnp.where(outer_valid, 0.0, NEG)
            query_t, grad_t = (
                jnp.concatenate(
                    [
                        jnp.transpose(
                            side_in[
                                head,
                                i,
                                (member * 2 + block) * 256 : (member * 2 + block) * 256 + 256,
                            ]
                        )
                        for i in range(2)
                    ],
                    axis=1,
                )
                for member in range(2)
            )
            wait_unit(unit)
            peak = jnp.full((8, ROWS), NEG, F32)
            for slot in range(SLOTS):
                part = dot(keys[span_of(slot)], query_t, 1, 0)
                if slot == side:
                    part = part + width_bias
                if slot == 2:
                    part = part + outer_bias
                score[span_of(slot)] = part
                peak = jnp.maximum(peak, jnp.max(part.reshape(BLOCK // 8, 8, ROWS), axis=0))
                yield
            state["peak"] = jnp.max(peak, axis=0, keepdims=True) * log_scale
            state["query_t"], state["grad_t"] = query_t, grad_t
            yield

        def weight_stage():
            total = jnp.zeros((8, ROWS), F32)
            for slot in range(SLOTS):
                part = jnp.exp2(score[span_of(slot)] * log_scale - state["peak"])
                total = total + jnp.sum(part.reshape(BLOCK // 8, 8, ROWS), axis=0)
                weight[span_of(slot)] = part.astype(BF16)
                yield
            state["inverse"] = 1.0 / jnp.sum(total, axis=0, keepdims=True)
            yield

        def out_stage():
            out_t = (dot(values[...], weight[...], 0, 0) * state["inverse"]).astype(BF16)
            grad_t = (state["grad_t"].astype(F32) * state["inverse"]).astype(BF16)
            state["delta"] = jnp.sum(
                out_t.astype(F32) * grad_t.astype(F32), axis=0, keepdims=True
            )
            state["grad_t"], state["out_t"] = grad_t, out_t
            yield

        def dscore_stage():
            for slot in range(SLOTS):
                part = dot(values[span_of(slot)], state["grad_t"], 1, 0)
                dscore[span_of(slot)] = (
                    weight[span_of(slot)].astype(F32) * (part - state["delta"])
                ).astype(BF16)
                yield

        def term_stage():
            dquery_t = (dot(keys[...], dscore[...], 0, 0) * scale).astype(BF16)
            for member, rows_t in enumerate((state["out_t"], dquery_t)):
                first = (member * 2 + block) * 256
                for i in range(2):
                    side_store[head, i, first : first + 256] = jnp.transpose(
                        rows_t[:, i * 256 : i * 256 + 256]
                    )
            if block == 1:
                for i in range(2):
                    side_out(head, i).start()
            yield
            from_ext = even if block == 0 else odd
            targets = [0, 1, jnp.where(from_ext, 2, 3 + side)]
            targets += [3 + 2 * level + chosen(block, level) for level in range(LEVELS)]
            for member, (lhs, rhs, factor) in enumerate(
                ((dscore, state["query_t"], scale), (weight, state["grad_t"], None))
            ):
                for pair in range(SLOTS // 2):
                    terms = dot(lhs[span_of(pair * 2, 2)], rhs, 1, 1)
                    if factor is not None:
                        terms = terms * factor
                    for inner in range(2):
                        row = targets[pair * 2 + inner] * BLOCK
                        if pair:
                            row = pl.multiple_of(row, BLOCK)
                        acc[head, member, pl.ds(row, BLOCK)] += terms[span_of(inner)]
                    yield
                if block == 1:
                    ext_store[head, member] = acc[head, member, span_of(2)].astype(BF16)
                    for level in range(LEVELS):
                        level_store[head, level, member] = acc[
                            head, member, span_of(3 + 2 * level, 2)
                        ].astype(BF16)
                    for copy in term_copies(head, member):
                        copy.start()
                    yield

        return score_stage(), weight_stage(), out_stage(), dscore_stage(), term_stage()

    def emit(*stages):
        running = list(stages)
        while running:
            running = [stage for stage in running if next(stage, stage) is not stage]

    units = 2 * PER
    for copy in side_copies(0):
        copy.start()
    start_unit(0)
    acc[...] = jnp.zeros_like(acc)
    stages = [unit_stages(unit) for unit in range(units)]
    emit(stages[0][0])
    for head in range(1, PER):
        for copy in side_copies(head):
            copy.start()
    for unit in range(units):
        if unit + 1 < units:
            start_unit(unit + 1)
        emit(stages[unit][1])
        emit(stages[unit][2])
        emit(stages[unit][3])
        emit(stages[unit][4])
        if unit + 1 < units:
            emit(stages[unit + 1][0])
    for head in range(PER):
        for i in range(2):
            side_out(head, i).wait()
        for member in range(2):
            for copy in term_copies(head, member):
                copy.wait()


def attend_scratch(rows):
    return [
        pltpu.VMEM((2, SLOTS * BLOCK, ROWS), F32),
        pltpu.VMEM((2, SLOTS * BLOCK, ROWS), BF16),
        pltpu.VMEM((2, SLOTS * BLOCK, ROWS), BF16),
        pltpu.VMEM((2 * PER, 2, SLOTS * BLOCK, HEAD_DIM), BF16),
        pltpu.VMEM((PER, 2, 1040, HEAD_DIM), BF16),
        pltpu.VMEM((PER, 2, 1024, HEAD_DIM), BF16),
        pltpu.VMEM((PER, 2, (3 + 2 * LEVELS) * BLOCK, HEAD_DIM), F32),
        pltpu.VMEM((PER, 2, BLOCK, HEAD_DIM), BF16),
        pltpu.VMEM((PER, LEVELS, 2, rows, HEAD_DIM), BF16),
        pltpu.SemaphoreType.DMA((2 * PER,)),
        pltpu.SemaphoreType.DMA((PER, 2)),
        pltpu.SemaphoreType.DMA((PER, 3, 2 + LEVELS)),
    ]


def finish_sides_kernel(scalars, *refs):
    sources, targets = refs[:-2], refs[-2:]
    order = query_order(scalars[0], 1)
    for member, target in enumerate(targets):
        for part in range(16):
            block, inner = part // 8, (part % 8) * 16
            pieces = []
            for head in range(2 * LOCAL_HEADS):
                local = head % LOCAL_HEADS
                source = sources[(head // LOCAL_HEADS) * CHUNKS + local // PER]
                for group in range(2):
                    start = (member * 2 + block) * 256 + group * 128 + inner
                    pieces.append(source[local % PER, start : start + 16])
            rows = jnp.concatenate(pieces, axis=0)
            target[part * 256 : part * 256 + 256] = dot(order, rows, 1, 0).astype(BF16)


def finish_pairs_kernel(scalars, *refs):
    even = scalars[0] == 0
    count = (len(refs) - 3) // 2
    far, targets, ins, sems = refs[:count], refs[count : count + 2], refs[count + 2 : -1], refs[-1]
    copies = [
        pltpu.make_async_copy(source, store, sems.at[i])
        for i, (source, store) in enumerate(zip(far, ins))
    ]
    for copy in copies:
        copy.start()
    for copy in copies:
        copy.wait()
    beyond, whole, split = ins[0], ins[1:4], ins[4:]
    order = key_order(1)
    for member, target in enumerate(targets):
        for part in range(4):
            span = slice(part * 64, part * 64 + 64)
            inner = slice((part % 2) * 64, (part % 2) * 64 + 64)
            pieces = []
            for head in range(LOCAL_HEADS):
                total = beyond[head, member, inner].astype(F32)
                total = jnp.where(even if part < 2 else jnp.logical_not(even), total, 0.0)
                for ref in whole:
                    total = total + ref[head, member, span].astype(F32)
                for ref in split[head // PER :: CHUNKS]:
                    total = total + ref[head % PER, member, span].astype(F32)
                pieces.append(total.astype(BF16))
            rows = jnp.concatenate(pieces, axis=0)
            target[part * 256 : part * 256 + 256] = dot(order, rows, 1, 0).astype(BF16)


def flipped(value, mask):
    return lax.ppermute(value, "seq", [(i, i ^ mask) for i in range(lax.axis_size("seq"))])


def past_end(value):
    pairs = []
    for i in range(1, lax.axis_size("seq") - 1, 2):
        pairs += [(i, i + 1), (i + 1, i)]
    return lax.ppermute(value, "seq", pairs)


def other_head(value):
    return lax.ppermute(value, "head", [(0, 1), (1, 0)])


def added(first, second):
    return (first.astype(F32) + second.astype(F32)).astype(BF16)


def shards(query, key_in, value, grad_out, band_width, stride_bits, partner_table):
    rows = key_in.shape[0]
    device = lax.axis_index("seq").astype(jnp.int32)
    place = lax.axis_index("head").astype(jnp.int32)
    odd = device & 1
    match = (stride_bits[None, :] == jnp.arange(LEVELS, dtype=jnp.int32)[:, None]).astype(jnp.int32)
    chosen = jnp.sum(partner_table[:, None, :] * match[None], axis=2)
    scalars = jnp.concatenate(
        [device[None], jnp.full((1,), lax.axis_size("seq") - 1, jnp.int32), chosen.reshape(-1)]
    )

    whole = jax.ShapeDtypeStruct((LOCAL_HEADS, 2, rows, HEAD_DIM), BF16)
    pair = jax.ShapeDtypeStruct((PER, 2, rows, HEAD_DIM), BF16)
    padded = jax.ShapeDtypeStruct((PER, 2, rows + PAD, HEAD_DIM), BF16)
    terms = jax.ShapeDtypeStruct((PER, 2, rows, HEAD_DIM), F32)
    ends = jax.ShapeDtypeStruct((LOCAL_HEADS, 2, BLOCK, HEAD_DIM), BF16)
    sides = jax.ShapeDtypeStruct((PER, 1040, HEAD_DIM), BF16)
    half = jax.ShapeDtypeStruct((PER, 1024, HEAD_DIM), BF16)

    own, own_a, own_b, own_end = pl.pallas_call(
        pack_pairs_kernel,
        out_shape=[whole, padded, padded, ends],
        in_specs=[SCALARS] + [FAR] * 2,
        out_specs=[WHOLE] * 4,
        scratch_shapes=[pltpu.VMEM((rows * 4, HEAD_DIM), BF16)] * 2
        + [pltpu.SemaphoreType.DMA((2, 2))],
        compiler_params=vmem(PACK_MIB),
        name="pack_pairs",
    )(odd[None], key_in.reshape(-1, HEAD_DIM), value.reshape(-1, HEAD_DIM))

    z2_a = flipped(own_a, 32)
    z1_a = flipped(own_a, 16)
    y1 = flipped(own, 2)
    core = flipped(own, 1)
    x = flipped(own, 8)
    ext = past_end(lax.optimization_barrier((own_end, core))[0])
    keep_a, keep_b, send_a, send_b = pl.pallas_call(
        pack_sides_kernel,
        out_shape=[sides] * (2 * CHUNKS),
        in_specs=[SCALARS] + [FAR] * 3,
        out_specs=[WHOLE] * (2 * CHUNKS),
        scratch_shapes=[pltpu.VMEM((rows * 16, HEAD_DIM), BF16)] * 2
        + [pltpu.SemaphoreType.DMA((2, 4))],
        compiler_params=vmem(SIDES_MIB),
        name="pack_sides",
    )(
        jnp.concatenate([place[None], band_width.reshape(-1)]),
        query.reshape(-1, HEAD_DIM),
        grad_out.reshape(-1, HEAD_DIM),
        core,
    )
    to_z2, to_head = lax.optimization_barrier((own_b, send_a))
    z6_a = flipped(z2_a, 96)
    z2_b = flipped(to_z2, 32)
    other_a = other_head(to_head)
    y3 = flipped(y1, 6)
    to_head, to_z1 = lax.optimization_barrier((send_b, to_z2))
    z4_b = flipped(to_z1, 64)
    z1_b = flipped(to_z1, 16)
    other_b = other_head(to_head)

    def attend(chunk, mine, keep, other, z1, z2, z4, reused):
        ins = [scalars, mine, ext, core, y1, y3, x, z1, z2, z4, keep, other, *reused]
        outs = [half, half, terms, ends, *[whole] * 4, padded, padded, padded]
        return pl.pallas_call(
            functools.partial(attend_kernel, chunk * PER, len(reused)),
            out_shape=outs,
            in_specs=[SCALARS] + [FAR] * (len(ins) - 1),
            out_specs=[FAR] * len(outs),
            scratch_shapes=attend_scratch(rows),
            input_output_aliases={12 + i: 3 + i for i in range(len(reused))},
            compiler_params=vmem(ATT_MIB),
            cost_estimate=pl.CostEstimate(
                flops=PER * 2 * 12 * SLOTS * BLOCK * ROWS * HEAD_DIM,
                transcendentals=PER * 2 * SLOTS * BLOCK * ROWS,
                bytes_accessed=PER * 24 * rows * HEAD_DIM * 4,
            ),
            name="attend",
        )(*ins)

    first = attend(0, own_a, keep_a, other_a, z1_a, z2_a, z6_a, [])
    keep_out_a, other_out_a, terms_a = first[:3]
    z1_terms_a, z2_terms_a, z4_terms_a = first[8:]
    far_a = flipped(z4_terms_a, 96)
    swapped_a = other_head(other_out_a)
    back_z1_a = flipped(z1_terms_a, 16)
    second = attend(1, own_b, keep_b, other_b, z1_b, z2_b, z4_b, first[3:8])
    keep_out_b, other_out_b, terms_b, ext_terms, core_terms, y1_terms, y2_terms = second[:7]
    x_terms, z1_terms_b, z2_terms_b, z4_terms_b = second[7:]
    to_z6, to_y3, to_x, to_ext, far_a, swapped_a, back_z1_a = lax.optimization_barrier(
        (z4_terms_b, y2_terms, x_terms, ext_terms, far_a, swapped_a, back_z1_a)
    )
    far_b = flipped(to_z6, 96)
    back_z2_a = flipped(added(z2_terms_a, far_a), 32)
    near = flipped(to_y3, 6)
    back_x = flipped(to_x, 8)
    back_ext = past_end(to_ext)
    far_b, back_z2_a, near, back_x, back_ext, z1_terms_b, core_terms, other_out_b = (
        lax.optimization_barrier(
            (far_b, back_z2_a, near, back_x, back_ext, z1_terms_b, core_terms, other_out_b)
        )
    )
    back_z2_b = flipped(added(z2_terms_b, far_b), 32)
    back_y = flipped(added(y1_terms, near), 2)
    swapped_b = other_head(other_out_b)
    back_z1_b = flipped(z1_terms_b, 16)
    back_core = flipped(core_terms, 1)

    out, dquery = pl.pallas_call(
        finish_sides_kernel,
        out_shape=[jax.ShapeDtypeStruct((rows * 16, HEAD_DIM), BF16)] * 2,
        in_specs=[SCALARS] + [WHOLE] * (2 * CHUNKS),
        out_specs=[WHOLE] * 2,
        compiler_params=vmem(8),
        name="finish_sides",
    )(place[None], keep_out_a, keep_out_b, swapped_a, swapped_b)
    sums = [back_ext, back_core, back_y, back_x, terms_a, terms_b]
    sums += [back_z1_a, back_z1_b, back_z2_a, back_z2_b]
    dkey, dvalue = pl.pallas_call(
        finish_pairs_kernel,
        out_shape=[jax.ShapeDtypeStruct((rows * 4, HEAD_DIM), BF16)] * 2,
        in_specs=[SCALARS] + [FAR] * len(sums),
        out_specs=[WHOLE] * 2,
        scratch_shapes=[pltpu.VMEM(part.shape, part.dtype) for part in sums]
        + [pltpu.SemaphoreType.DMA((len(sums),))],
        compiler_params=vmem(16),
        name="finish_pairs",
    )(odd[None], *sums)
    return (
        out.reshape(query.shape),
        dquery.reshape(query.shape),
        dkey.reshape(key_in.shape),
        dvalue.reshape(key_in.shape),
    )


def solution(mesh):
    placed = (
        P("seq", None, "head", None),
        P("seq", "head", None),
        P("seq", "head", None),
        P("seq", None, "head", None),
        P(None, "head"),
        P(),
        P("seq", None),
    )
    return jax.shard_map(
        shards,
        mesh=mesh,
        in_specs=placed,
        out_specs=(
            P("seq", None, "head", None),
            P("seq", None, "head", None),
            P("seq", "head", None),
            P("seq", "head", None),
        ),
        check_vma=False,
    )
```

```python
import functools
import math

import jax
import jax.numpy as jnp
from jax import lax
from jax.experimental import pallas as pl
from jax.experimental.pallas import tpu as pltpu
from jax.sharding import PartitionSpec as P

BLOCK = 128
HEAD_DIM = 128
CHUNKS = 2
LOCAL_HEADS = 4
PER = LOCAL_HEADS // CHUNKS
LEVELS = 7
BAND_SLOTS = 3
SLOTS = BAND_SLOTS + LEVELS
ROWS = 512
PAD = 8
PACK_MIB = 56
SIDES_MIB = 8
ATT_MIB = 18
NEG = -1e30
F32 = jnp.float32
BF16 = jnp.bfloat16
WHOLE = pl.BlockSpec(memory_space=pltpu.VMEM)
FAR = pl.BlockSpec(memory_space=pltpu.HBM)
SCALARS = pl.BlockSpec(memory_space=pltpu.SMEM)


def vmem(mib):
    return pltpu.CompilerParams(vmem_limit_bytes=mib << 20)


def dot(lhs, rhs, lhs_dim, rhs_dim):
    return lax.dot_general(
        lhs, rhs, (((lhs_dim,), (rhs_dim,)), ((), ())), preferred_element_type=F32
    )


def query_order(place, rows_first):
    ordered = lax.broadcasted_iota(jnp.int32, (256, 256), rows_first)
    natural = lax.broadcasted_iota(jnp.int32, (256, 256), 1 - rows_first)
    source = (ordered & 15) * 16 + ((ordered >> 4) ^ (place * 8))
    return (natural == source).astype(BF16)


def key_order(rows_first):
    ordered = lax.broadcasted_iota(jnp.int32, (256, 256), rows_first)
    natural = lax.broadcasted_iota(jnp.int32, (256, 256), 1 - rows_first)
    return (natural == (ordered & 63) * 4 + (ordered >> 6)).astype(BF16)


def pieces_of(ref, store, sems, count):
    rows = ref.shape[0] // count
    copies = [
        pltpu.make_async_copy(
            ref.at[pl.ds(i * rows, rows)], store.at[pl.ds(i * rows, rows)], sems.at[i]
        )
        for i in range(count)
    ]
    for copy in copies:
        copy.start()
    return copies


def pack_pairs_kernel(scalars, key, value, *refs):
    whole, first, second, ends, key_in, value_in, sems = refs
    even = scalars[0] == 0
    copies = [
        pieces_of(ref, store, sems.at[member], 2)
        for member, (ref, store) in enumerate(((key, key_in), (value, value_in)))
    ]
    order = key_order(0)
    for block in range(2):
        for member, store in enumerate((key_in, value_in)):
            copies[member][block].wait()
            for inner in (0, 64):
                start = block * 512 + inner * 4
                rows = dot(order, store[start : start + 256], 1, 0).astype(BF16)
                span = slice(block * BLOCK + inner, block * BLOCK + inner + 64)
                end = slice(inner, inner + 64)
                for head in range(LOCAL_HEADS):
                    piece = rows[head * 64 : head * 64 + 64]
                    whole[head, member, span] = piece
                    (first, second)[head // PER][head % PER, member, span] = piece
                    if block == 0:
                        ends[head, member, end] = piece
                    else:
                        ends[head, member, end] = jnp.where(even, ends[head, member, end], piece)


def pack_sides_kernel(scalars, query, grad, unused, *refs):
    place = scalars[0]
    keeps, sends = refs[:CHUNKS], refs[CHUNKS : 2 * CHUNKS]
    stores, sems = refs[2 * CHUNKS : 2 * CHUNKS + 2], refs[2 * CHUNKS + 2]
    copies = [
        pieces_of(ref, store, sems.at[member], 4)
        for member, (ref, store) in enumerate(zip((query, grad), stores))
    ]
    order = query_order(place, 0)
    for part in range(16):
        for member, store in enumerate(stores):
            if part % 4 == 0:
                copies[member][part // 4].wait()
            rows = dot(order, store[part * 256 : part * 256 + 256], 1, 0).astype(BF16)
            block, inner = part // 8, (part % 8) * 16
            for head in range(2 * LOCAL_HEADS):
                target = (keeps, sends)[head // LOCAL_HEADS]
                local = head % LOCAL_HEADS
                for group in range(2):
                    start = (member * 2 + block) * 256 + group * 128 + inner
                    first = (head * 2 + group) * 16
                    target[local // PER][local % PER, start : start + 16] = rows[first : first + 16]
    sublane = lax.broadcasted_iota(jnp.int32, (16, HEAD_DIM), 0)
    for head in range(2 * LOCAL_HEADS):
        target = (keeps, sends)[head // LOCAL_HEADS]
        local = head % LOCAL_HEADS
        actual = head ^ (place * LOCAL_HEADS)
        width = jnp.where(sublane == 0, scalars[1 + actual * 2], scalars[2 + actual * 2])
        target[local // PER][local % PER, 1024:1040] = width.astype(F32).astype(BF16)


def attend_kernel(base, reused, scalars, *refs):
    own, ext = refs[:2]
    arrived = refs[2 : 2 + LEVELS]
    sides = refs[2 + LEVELS : 4 + LEVELS]
    refs = refs[4 + LEVELS + reused :]
    side_outs, terms_out, ext_out = refs[:2], refs[2], refs[3]
    level_outs = refs[4 : 4 + LEVELS]
    (scores, exps, dscores, pairs, side_in, side_store, acc, ext_store, level_store) = refs[
        4 + LEVELS : 13 + LEVELS
    ]
    pair_sems, side_sems, out_sems = refs[13 + LEVELS :]
    device = scalars[0]
    last = scalars[1]
    even = (device & 1) == 0
    odd = jnp.logical_not(even)
    scale = HEAD_DIM**-0.5
    log_scale = scale * math.log2(math.e)

    def chosen(block, level):
        return scalars[2 + block * LEVELS + level]

    def at_head(ref, head):
        return ref.at[head + base if ref.shape[0] == LOCAL_HEADS else head]

    def copy_pair(head, block, source, slot, count):
        unit = head * 2 + block
        return pltpu.make_async_copy(
            source,
            pairs.at[unit, :, pl.ds(slot * BLOCK, count * BLOCK)],
            pair_sems.at[unit],
        )

    def side_copies(head):
        return [
            pltpu.make_async_copy(sides[i].at[head], side_in.at[head, i], side_sems.at[head, i])
            for i in range(2)
        ]

    for head in range(PER):
        for copy in side_copies(head):
            copy.start()
        for block in range(2):
            side = 1 - block
            from_ext = even if block == 0 else odd
            copy_pair(head, block, at_head(own, head).at[:, pl.ds(0, 2 * BLOCK)], 0, 2).start()
            pl.when(from_ext)(copy_pair(head, block, at_head(ext, head), 2, 1).start)
            nearby = at_head(arrived[0], head).at[:, pl.ds(side * BLOCK, BLOCK)]
            pl.when(jnp.logical_not(from_ext))(copy_pair(head, block, nearby, 2, 1).start)
            for level in range(LEVELS):
                at = pl.ds(pl.multiple_of(chosen(block, level) * BLOCK, BLOCK), BLOCK)
                source = at_head(arrived[level], head).at[:, at]
                copy_pair(head, block, source, BAND_SLOTS + level, 1).start()

    def out_copies(head):
        copies = [(side_store.at[head, i], side_outs[i].at[head]) for i in range(2)]
        copies.append((acc.at[head, :, pl.ds(0, 2 * BLOCK)], at_head(terms_out, head)))
        copies.append((ext_store.at[head], at_head(ext_out, head)))
        copies += [
            (level_store.at[head, level], at_head(level_outs[level], head).at[:, pl.ds(0, 2 * BLOCK)])
            for level in range(LEVELS)
        ]
        return [
            pltpu.make_async_copy(source, target, out_sems.at[head, i])
            for i, (source, target) in enumerate(copies)
        ]

    def one_head(head, carry):
        acc[head] = jnp.zeros(acc.shape[1:], F32)
        for copy in side_copies(head):
            copy.wait()
        widths = jnp.concatenate(
            [
                side_in[head, i, 1024:1040].astype(F32)[group : group + 1]
                for i in range(2)
                for group in range(2)
            ],
            axis=1,
        )
        width_bias = jnp.where(widths > 1.5, 0.0, NEG)
        for block in range(2):
            unit = head * 2 + block
            side = 1 - block
            outer_valid = device > 0 if block == 0 else device < last
            from_ext = even if block == 0 else odd
            query_t, grad_t = (
                jnp.concatenate(
                    [
                        jnp.transpose(
                            side_in[
                                head,
                                i,
                                (member * 2 + block) * 256 : (member * 2 + block) * 256 + 256,
                            ]
                        )
                        for i in range(2)
                    ],
                    axis=1,
                )
                for member in range(2)
            )
            copy_pair(head, block, at_head(own, head).at[:, pl.ds(0, 2 * BLOCK)], 0, 2).wait()
            for slot in range(2, SLOTS):
                copy_pair(head, block, at_head(ext, head), slot, 1).wait()
            keys, values = pairs.at[unit, 0], pairs.at[unit, 1]
            outer_bias = width_bias + jnp.where(outer_valid, 0.0, NEG)
            peak = jnp.full((8, ROWS), NEG, F32)
            for slot in range(SLOTS):
                span = slice(slot * BLOCK, slot * BLOCK + BLOCK)
                part = dot(keys[span], query_t, 1, 0)
                if slot == side:
                    part = part + width_bias
                if slot == 2:
                    part = part + outer_bias
                scores[span] = part
                peak = jnp.maximum(peak, jnp.max(part.reshape(BLOCK // 8, 8, ROWS), axis=0))
            peak = jnp.max(peak, axis=0, keepdims=True) * log_scale
            total = jnp.zeros((8, ROWS), F32)
            for slot in range(SLOTS):
                span = slice(slot * BLOCK, slot * BLOCK + BLOCK)
                part = jnp.exp2(scores[span] * log_scale - peak)
                total = total + jnp.sum(part.reshape(BLOCK // 8, 8, ROWS), axis=0)
                exps[span] = part.astype(BF16)
            inverse = 1.0 / jnp.sum(total, axis=0, keepdims=True)
            out_t = (dot(values[...], exps[...], 0, 0) * inverse).astype(BF16)
            grad_t = (grad_t.astype(F32) * inverse).astype(BF16)
            delta = jnp.sum(out_t.astype(F32) * grad_t.astype(F32), axis=0, keepdims=True)
            for slot in range(SLOTS):
                span = slice(slot * BLOCK, slot * BLOCK + BLOCK)
                part = dot(values[span], grad_t, 1, 0)
                dscores[span] = (exps[span].astype(F32) * (part - delta)).astype(BF16)
            dquery_t = (dot(keys[...], dscores[...], 0, 0) * scale).astype(BF16)
            for member, rows_t in enumerate((out_t, dquery_t)):
                first = (member * 2 + block) * 256
                for i in range(2):
                    side_store[head, i, first : first + 256] = jnp.transpose(
                        rows_t[:, i * 256 : i * 256 + 256]
                    )
            outer_row = jnp.where(from_ext, 2, 3 + side)
            for member, (lhs, rhs, factor) in enumerate(
                ((dscores, query_t, scale), (exps, grad_t, None))
            ):
                terms = dot(lhs[...], rhs, 1, 1)
                if factor is not None:
                    terms = terms * factor
                acc[head, member, 0 : 2 * BLOCK] += terms[0 : 2 * BLOCK]
                targets = [outer_row] + [
                    3 + 2 * level + chosen(block, level) for level in range(LEVELS)
                ]
                for slot, row in enumerate(targets):
                    at = pl.ds(pl.multiple_of(row * BLOCK, BLOCK), BLOCK)
                    first = (2 + slot) * BLOCK
                    acc[head, member, at] += terms[first : first + BLOCK]
        for member in range(2):
            ext_store[head, member] = acc[head, member, 2 * BLOCK : 3 * BLOCK].astype(BF16)
            for level in range(LEVELS):
                first = (3 + 2 * level) * BLOCK
                level_store[head, level, member] = acc[
                    head, member, first : first + 2 * BLOCK
                ].astype(BF16)
        for copy in out_copies(head):
            copy.start()
        return carry

    lax.fori_loop(0, PER, one_head, 0)
    for head in range(PER):
        for copy in out_copies(head):
            copy.wait()


def attend_scratch(rows):
    return [
        pltpu.VMEM((SLOTS * BLOCK, ROWS), F32),
        pltpu.VMEM((SLOTS * BLOCK, ROWS), BF16),
        pltpu.VMEM((SLOTS * BLOCK, ROWS), BF16),
        pltpu.VMEM((2 * PER, 2, SLOTS * BLOCK, HEAD_DIM), BF16),
        pltpu.VMEM((PER, 2, 1040, HEAD_DIM), BF16),
        pltpu.VMEM((PER, 2, 1024, HEAD_DIM), BF16),
        pltpu.VMEM((PER, 2, (3 + 2 * LEVELS) * BLOCK, HEAD_DIM), F32),
        pltpu.VMEM((PER, 2, BLOCK, HEAD_DIM), BF16),
        pltpu.VMEM((PER, LEVELS, 2, rows, HEAD_DIM), BF16),
        pltpu.SemaphoreType.DMA((2 * PER,)),
        pltpu.SemaphoreType.DMA((PER, 2)),
        pltpu.SemaphoreType.DMA((PER, 4 + LEVELS)),
    ]


def finish_sides_kernel(scalars, *refs):
    sources, targets = refs[:-2], refs[-2:]
    order = query_order(scalars[0], 1)
    for member, target in enumerate(targets):
        for part in range(16):
            block, inner = part // 8, (part % 8) * 16
            pieces = []
            for head in range(2 * LOCAL_HEADS):
                local = head % LOCAL_HEADS
                source = sources[(head // LOCAL_HEADS) * CHUNKS + local // PER]
                for group in range(2):
                    start = (member * 2 + block) * 256 + group * 128 + inner
                    pieces.append(source[local % PER, start : start + 16])
            rows = jnp.concatenate(pieces, axis=0)
            target[part * 256 : part * 256 + 256] = dot(order, rows, 1, 0).astype(BF16)


def finish_pairs_kernel(scalars, *refs):
    even = scalars[0] == 0
    count = (len(refs) - 3) // 2
    far, targets, ins, sems = refs[:count], refs[count : count + 2], refs[count + 2 : -1], refs[-1]
    copies = [
        pltpu.make_async_copy(source, store, sems.at[i])
        for i, (source, store) in enumerate(zip(far, ins))
    ]
    for copy in copies:
        copy.start()
    for copy in copies:
        copy.wait()
    beyond, whole, split = ins[0], ins[1:4], ins[4:]
    order = key_order(1)
    for member, target in enumerate(targets):
        for part in range(4):
            span = slice(part * 64, part * 64 + 64)
            inner = slice((part % 2) * 64, (part % 2) * 64 + 64)
            pieces = []
            for head in range(LOCAL_HEADS):
                total = beyond[head, member, inner].astype(F32)
                total = jnp.where(even if part < 2 else jnp.logical_not(even), total, 0.0)
                for ref in whole:
                    total = total + ref[head, member, span].astype(F32)
                for ref in split[head // PER :: CHUNKS]:
                    total = total + ref[head % PER, member, span].astype(F32)
                pieces.append(total.astype(BF16))
            rows = jnp.concatenate(pieces, axis=0)
            target[part * 256 : part * 256 + 256] = dot(order, rows, 1, 0).astype(BF16)


def flipped(value, mask):
    return lax.ppermute(value, "seq", [(i, i ^ mask) for i in range(lax.axis_size("seq"))])


def past_end(value):
    pairs = []
    for i in range(1, lax.axis_size("seq") - 1, 2):
        pairs += [(i, i + 1), (i + 1, i)]
    return lax.ppermute(value, "seq", pairs)


def other_head(value):
    return lax.ppermute(value, "head", [(0, 1), (1, 0)])


def added(first, second):
    return (first.astype(F32) + second.astype(F32)).astype(BF16)


def shards(query, key_in, value, grad_out, band_width, stride_bits, partner_table):
    rows = key_in.shape[0]
    device = lax.axis_index("seq").astype(jnp.int32)
    place = lax.axis_index("head").astype(jnp.int32)
    odd = device & 1
    match = (stride_bits[None, :] == jnp.arange(LEVELS, dtype=jnp.int32)[:, None]).astype(jnp.int32)
    chosen = jnp.sum(partner_table[:, None, :] * match[None], axis=2)
    scalars = jnp.concatenate(
        [device[None], jnp.full((1,), lax.axis_size("seq") - 1, jnp.int32), chosen.reshape(-1)]
    )

    whole = jax.ShapeDtypeStruct((LOCAL_HEADS, 2, rows, HEAD_DIM), BF16)
    pair = jax.ShapeDtypeStruct((PER, 2, rows, HEAD_DIM), BF16)
    padded = jax.ShapeDtypeStruct((PER, 2, rows + PAD, HEAD_DIM), BF16)
    terms = jax.ShapeDtypeStruct((PER, 2, rows, HEAD_DIM), F32)
    ends = jax.ShapeDtypeStruct((LOCAL_HEADS, 2, BLOCK, HEAD_DIM), BF16)
    sides = jax.ShapeDtypeStruct((PER, 1040, HEAD_DIM), BF16)
    half = jax.ShapeDtypeStruct((PER, 1024, HEAD_DIM), BF16)

    own, own_a, own_b, own_end = pl.pallas_call(
        pack_pairs_kernel,
        out_shape=[whole, padded, padded, ends],
        in_specs=[SCALARS] + [FAR] * 2,
        out_specs=[WHOLE] * 4,
        scratch_shapes=[pltpu.VMEM((rows * 4, HEAD_DIM), BF16)] * 2
        + [pltpu.SemaphoreType.DMA((2, 2))],
        compiler_params=vmem(PACK_MIB),
        name="pack_pairs",
    )(odd[None], key_in.reshape(-1, HEAD_DIM), value.reshape(-1, HEAD_DIM))

    z2_a = flipped(own_a, 32)
    z1_a = flipped(own_a, 16)
    y1 = flipped(own, 2)
    core = flipped(own, 1)
    x = flipped(own, 8)
    ext = past_end(lax.optimization_barrier((own_end, core))[0])
    keep_a, keep_b, send_a, send_b = pl.pallas_call(
        pack_sides_kernel,
        out_shape=[sides] * (2 * CHUNKS),
        in_specs=[SCALARS] + [FAR] * 3,
        out_specs=[WHOLE] * (2 * CHUNKS),
        scratch_shapes=[pltpu.VMEM((rows * 16, HEAD_DIM), BF16)] * 2
        + [pltpu.SemaphoreType.DMA((2, 4))],
        compiler_params=vmem(SIDES_MIB),
        name="pack_sides",
    )(
        jnp.concatenate([place[None], band_width.reshape(-1)]),
        query.reshape(-1, HEAD_DIM),
        grad_out.reshape(-1, HEAD_DIM),
        core,
    )
    to_z2, to_head = lax.optimization_barrier((own_b, send_a))
    z6_a = flipped(z2_a, 96)
    z2_b = flipped(to_z2, 32)
    other_a = other_head(to_head)
    y3 = flipped(y1, 6)
    to_head, to_z1 = lax.optimization_barrier((send_b, to_z2))
    z4_b = flipped(to_z1, 64)
    z1_b = flipped(to_z1, 16)
    other_b = other_head(to_head)

    def attend(chunk, mine, keep, other, z1, z2, z4, reused):
        ins = [scalars, mine, ext, core, y1, y3, x, z1, z2, z4, keep, other, *reused]
        outs = [half, half, terms, ends, *[whole] * 4, padded, padded, padded]
        return pl.pallas_call(
            functools.partial(attend_kernel, chunk * PER, len(reused)),
            out_shape=outs,
            in_specs=[SCALARS] + [FAR] * (len(ins) - 1),
            out_specs=[FAR] * len(outs),
            scratch_shapes=attend_scratch(rows),
            input_output_aliases={12 + i: 3 + i for i in range(len(reused))},
            compiler_params=vmem(ATT_MIB),
            cost_estimate=pl.CostEstimate(
                flops=PER * 2 * 12 * SLOTS * BLOCK * ROWS * HEAD_DIM,
                transcendentals=PER * 2 * SLOTS * BLOCK * ROWS,
                bytes_accessed=PER * 24 * rows * HEAD_DIM * 4,
            ),
            name="attend",
        )(*ins)

    first = attend(0, own_a, keep_a, other_a, z1_a, z2_a, z6_a, [])
    keep_out_a, other_out_a, terms_a = first[:3]
    z1_terms_a, z2_terms_a, z4_terms_a = first[8:]
    far_a = flipped(z4_terms_a, 96)
    swapped_a = other_head(other_out_a)
    back_z1_a = flipped(z1_terms_a, 16)
    second = attend(1, own_b, keep_b, other_b, z1_b, z2_b, z4_b, first[3:8])
    keep_out_b, other_out_b, terms_b, ext_terms, core_terms, y1_terms, y2_terms = second[:7]
    x_terms, z1_terms_b, z2_terms_b, z4_terms_b = second[7:]
    to_z6, to_y3, to_x, to_ext, to_core, far_a, swapped_a, back_z1_a = lax.optimization_barrier(
        (z4_terms_b, y2_terms, x_terms, ext_terms, core_terms, far_a, swapped_a, back_z1_a)
    )
    far_b = flipped(to_z6, 96)
    back_z2_a = flipped(added(z2_terms_a, far_a), 32)
    near = flipped(to_y3, 6)
    back_core = flipped(to_core, 1)
    back_x = flipped(to_x, 8)
    back_ext = past_end(lax.optimization_barrier((to_ext, back_core))[0])
    far_b, back_z2_a, near, back_x, back_ext, z1_terms_b, other_out_b = lax.optimization_barrier(
        (far_b, back_z2_a, near, back_x, back_ext, z1_terms_b, other_out_b)
    )
    back_z2_b = flipped(added(z2_terms_b, far_b), 32)
    back_y = flipped(added(y1_terms, near), 2)
    swapped_b = other_head(other_out_b)
    back_z1_b = flipped(z1_terms_b, 16)

    out, dquery = pl.pallas_call(
        finish_sides_kernel,
        out_shape=[jax.ShapeDtypeStruct((rows * 16, HEAD_DIM), BF16)] * 2,
        in_specs=[SCALARS] + [WHOLE] * (2 * CHUNKS),
        out_specs=[WHOLE] * 2,
        compiler_params=vmem(8),
        name="finish_sides",
    )(place[None], keep_out_a, keep_out_b, swapped_a, swapped_b)
    sums = [back_ext, back_core, back_y, back_x, terms_a, terms_b]
    sums += [back_z1_a, back_z1_b, back_z2_a, back_z2_b]
    dkey, dvalue = pl.pallas_call(
        finish_pairs_kernel,
        out_shape=[jax.ShapeDtypeStruct((rows * 4, HEAD_DIM), BF16)] * 2,
        in_specs=[SCALARS] + [FAR] * len(sums),
        out_specs=[WHOLE] * 2,
        scratch_shapes=[pltpu.VMEM(part.shape, part.dtype) for part in sums]
        + [pltpu.SemaphoreType.DMA((len(sums),))],
        compiler_params=vmem(16),
        name="finish_pairs",
    )(odd[None], *sums)
    return (
        out.reshape(query.shape),
        dquery.reshape(query.shape),
        dkey.reshape(key_in.shape),
        dvalue.reshape(key_in.shape),
    )


def solution(mesh):
    placed = (
        P("seq", None, "head", None),
        P("seq", "head", None),
        P("seq", "head", None),
        P("seq", None, "head", None),
        P(None, "head"),
        P(),
        P("seq", None),
    )
    return jax.shard_map(
        shards,
        mesh=mesh,
        in_specs=placed,
        out_specs=(
            P("seq", None, "head", None),
            P("seq", None, "head", None),
            P("seq", "head", None),
            P("seq", "head", None),
        ),
        check_vma=False,
    )
```

```python
import functools
import math

import jax
import jax.numpy as jnp
from jax import lax
from jax.experimental import pallas as pl
from jax.experimental.pallas import tpu as pltpu
from jax.sharding import PartitionSpec as P

BLOCK = 128
HEAD_DIM = 128
CHUNKS = 2
LOCAL_HEADS = 4
PER = LOCAL_HEADS // CHUNKS
LEVELS = 7
BAND_SLOTS = 3
SLOTS = BAND_SLOTS + LEVELS
ROWS = 512
PAD = 8
PACK_MIB = 56
SIDES_MIB = 8
ATT_MIB = 18
NEG = -1e30
F32 = jnp.float32
BF16 = jnp.bfloat16
WHOLE = pl.BlockSpec(memory_space=pltpu.VMEM)
FAR = pl.BlockSpec(memory_space=pltpu.HBM)
SCALARS = pl.BlockSpec(memory_space=pltpu.SMEM)


def vmem(mib):
    return pltpu.CompilerParams(vmem_limit_bytes=mib << 20)


def dot(lhs, rhs, lhs_dim, rhs_dim):
    return lax.dot_general(
        lhs, rhs, (((lhs_dim,), (rhs_dim,)), ((), ())), preferred_element_type=F32
    )


def query_order(place, rows_first):
    ordered = lax.broadcasted_iota(jnp.int32, (256, 256), rows_first)
    natural = lax.broadcasted_iota(jnp.int32, (256, 256), 1 - rows_first)
    source = (ordered & 15) * 16 + ((ordered >> 4) ^ (place * 8))
    return (natural == source).astype(BF16)


def key_order(rows_first):
    ordered = lax.broadcasted_iota(jnp.int32, (256, 256), rows_first)
    natural = lax.broadcasted_iota(jnp.int32, (256, 256), 1 - rows_first)
    return (natural == (ordered & 63) * 4 + (ordered >> 6)).astype(BF16)


def pieces_of(ref, store, sems, count):
    rows = ref.shape[0] // count
    copies = [
        pltpu.make_async_copy(
            ref.at[pl.ds(i * rows, rows)], store.at[pl.ds(i * rows, rows)], sems.at[i]
        )
        for i in range(count)
    ]
    for copy in copies:
        copy.start()
    return copies


def pack_pairs_kernel(scalars, key, value, *refs):
    whole, first, second, ends, key_in, value_in, sems = refs
    even = scalars[0] == 0
    copies = [
        pieces_of(ref, store, sems.at[member], 2)
        for member, (ref, store) in enumerate(((key, key_in), (value, value_in)))
    ]
    order = key_order(0)
    for block in range(2):
        for member, store in enumerate((key_in, value_in)):
            copies[member][block].wait()
            for inner in (0, 64):
                start = block * 512 + inner * 4
                rows = dot(order, store[start : start + 256], 1, 0).astype(BF16)
                span = slice(block * BLOCK + inner, block * BLOCK + inner + 64)
                end = slice(inner, inner + 64)
                for head in range(LOCAL_HEADS):
                    piece = rows[head * 64 : head * 64 + 64]
                    whole[head, member, span] = piece
                    (first, second)[head // PER][head % PER, member, span] = piece
                    if block == 0:
                        ends[head, member, end] = piece
                    else:
                        ends[head, member, end] = jnp.where(even, ends[head, member, end], piece)


def pack_sides_kernel(scalars, query, grad, unused, *refs):
    place = scalars[0]
    keeps, sends = refs[:CHUNKS], refs[CHUNKS : 2 * CHUNKS]
    stores, sems = refs[2 * CHUNKS : 2 * CHUNKS + 2], refs[2 * CHUNKS + 2]
    copies = [
        pieces_of(ref, store, sems.at[member], 4)
        for member, (ref, store) in enumerate(zip((query, grad), stores))
    ]
    order = query_order(place, 0)
    for part in range(16):
        for member, store in enumerate(stores):
            if part % 4 == 0:
                copies[member][part // 4].wait()
            rows = dot(order, store[part * 256 : part * 256 + 256], 1, 0).astype(BF16)
            block, inner = part // 8, (part % 8) * 16
            for head in range(2 * LOCAL_HEADS):
                target = (keeps, sends)[head // LOCAL_HEADS]
                local = head % LOCAL_HEADS
                for group in range(2):
                    start = (member * 2 + block) * 256 + group * 128 + inner
                    first = (head * 2 + group) * 16
                    target[local // PER][local % PER, start : start + 16] = rows[first : first + 16]
    sublane = lax.broadcasted_iota(jnp.int32, (16, HEAD_DIM), 0)
    for head in range(2 * LOCAL_HEADS):
        target = (keeps, sends)[head // LOCAL_HEADS]
        local = head % LOCAL_HEADS
        actual = head ^ (place * LOCAL_HEADS)
        width = jnp.where(sublane == 0, scalars[1 + actual * 2], scalars[2 + actual * 2])
        target[local // PER][local % PER, 1024:1040] = width.astype(F32).astype(BF16)


def attend_kernel(base, reused, scalars, *refs):
    own, ext = refs[:2]
    arrived = refs[2 : 2 + LEVELS]
    sides = refs[2 + LEVELS : 4 + LEVELS]
    refs = refs[4 + LEVELS + reused :]
    side_outs, terms_out, ext_out = refs[:2], refs[2], refs[3]
    level_outs = refs[4 : 4 + LEVELS]
    (scores, exps, dscores, pairs, side_in, side_store, acc, ext_store, level_store) = refs[
        4 + LEVELS : 13 + LEVELS
    ]
    pair_sems, side_sems, out_sems = refs[13 + LEVELS :]
    device = scalars[0]
    last = scalars[1]
    even = (device & 1) == 0
    odd = jnp.logical_not(even)
    scale = HEAD_DIM**-0.5
    log_scale = scale * math.log2(math.e)

    def chosen(block, level):
        return scalars[2 + block * LEVELS + level]

    def at_head(ref, head):
        return ref.at[head + base if ref.shape[0] == LOCAL_HEADS else head]

    def copy_pair(head, block, source, slot, count):
        unit = head * 2 + block
        return pltpu.make_async_copy(
            source,
            pairs.at[unit, :, pl.ds(slot * BLOCK, count * BLOCK)],
            pair_sems.at[unit],
        )

    def side_copies(head):
        return [
            pltpu.make_async_copy(sides[i].at[head], side_in.at[head, i], side_sems.at[head, i])
            for i in range(2)
        ]

    for head in range(PER):
        for copy in side_copies(head):
            copy.start()
        for block in range(2):
            side = 1 - block
            from_ext = even if block == 0 else odd
            copy_pair(head, block, at_head(own, head).at[:, pl.ds(0, 2 * BLOCK)], 0, 2).start()
            pl.when(from_ext)(copy_pair(head, block, at_head(ext, head), 2, 1).start)
            nearby = at_head(arrived[0], head).at[:, pl.ds(side * BLOCK, BLOCK)]
            pl.when(jnp.logical_not(from_ext))(copy_pair(head, block, nearby, 2, 1).start)
            for level in range(LEVELS):
                at = pl.ds(pl.multiple_of(chosen(block, level) * BLOCK, BLOCK), BLOCK)
                source = at_head(arrived[level], head).at[:, at]
                copy_pair(head, block, source, BAND_SLOTS + level, 1).start()

    def out_copies(head):
        copies = [(side_store.at[head, i], side_outs[i].at[head]) for i in range(2)]
        copies.append((acc.at[head, :, pl.ds(0, 2 * BLOCK)], at_head(terms_out, head)))
        copies.append((ext_store.at[head], at_head(ext_out, head)))
        copies += [
            (level_store.at[head, level], at_head(level_outs[level], head).at[:, pl.ds(0, 2 * BLOCK)])
            for level in range(LEVELS)
        ]
        return [
            pltpu.make_async_copy(source, target, out_sems.at[head, i])
            for i, (source, target) in enumerate(copies)
        ]

    def one_head(head, carry):
        acc[head] = jnp.zeros(acc.shape[1:], F32)
        for copy in side_copies(head):
            copy.wait()
        widths = jnp.concatenate(
            [
                side_in[head, i, 1024:1040].astype(F32)[group : group + 1]
                for i in range(2)
                for group in range(2)
            ],
            axis=1,
        )
        width_bias = jnp.where(widths > 1.5, 0.0, NEG)
        for block in range(2):
            unit = head * 2 + block
            side = 1 - block
            outer_valid = device > 0 if block == 0 else device < last
            from_ext = even if block == 0 else odd
            query_t, grad_t = (
                jnp.concatenate(
                    [
                        jnp.transpose(
                            side_in[
                                head,
                                i,
                                (member * 2 + block) * 256 : (member * 2 + block) * 256 + 256,
                            ]
                        )
                        for i in range(2)
                    ],
                    axis=1,
                )
                for member in range(2)
            )
            copy_pair(head, block, at_head(own, head).at[:, pl.ds(0, 2 * BLOCK)], 0, 2).wait()
            for slot in range(2, SLOTS):
                copy_pair(head, block, at_head(ext, head), slot, 1).wait()
            keys, values = pairs.at[unit, 0], pairs.at[unit, 1]
            outer_bias = width_bias + jnp.where(outer_valid, 0.0, NEG)
            peak = jnp.full((8, ROWS), NEG, F32)
            for slot in range(SLOTS):
                span = slice(slot * BLOCK, slot * BLOCK + BLOCK)
                part = dot(keys[span], query_t, 1, 0)
                if slot == side:
                    part = part + width_bias
                if slot == 2:
                    part = part + outer_bias
                scores[span] = part
                peak = jnp.maximum(peak, jnp.max(part.reshape(BLOCK // 8, 8, ROWS), axis=0))
            peak = jnp.max(peak, axis=0, keepdims=True) * log_scale
            total = jnp.zeros((8, ROWS), F32)
            for slot in range(SLOTS):
                span = slice(slot * BLOCK, slot * BLOCK + BLOCK)
                part = jnp.exp2(scores[span] * log_scale - peak)
                total = total + jnp.sum(part.reshape(BLOCK // 8, 8, ROWS), axis=0)
                exps[span] = part.astype(BF16)
            inverse = 1.0 / jnp.sum(total, axis=0, keepdims=True)
            out_t = (dot(values[...], exps[...], 0, 0) * inverse).astype(BF16)
            grad_t = (grad_t.astype(F32) * inverse).astype(BF16)
            delta = jnp.sum(out_t.astype(F32) * grad_t.astype(F32), axis=0, keepdims=True)
            for slot in range(SLOTS):
                span = slice(slot * BLOCK, slot * BLOCK + BLOCK)
                part = dot(values[span], grad_t, 1, 0)
                dscores[span] = (exps[span].astype(F32) * (part - delta)).astype(BF16)
            dquery_t = (dot(keys[...], dscores[...], 0, 0) * scale).astype(BF16)
            for member, rows_t in enumerate((out_t, dquery_t)):
                first = (member * 2 + block) * 256
                for i in range(2):
                    side_store[head, i, first : first + 256] = jnp.transpose(
                        rows_t[:, i * 256 : i * 256 + 256]
                    )
            outer_row = jnp.where(from_ext, 2, 3 + side)
            for member, (lhs, rhs, factor) in enumerate(
                ((dscores, query_t, scale), (exps, grad_t, None))
            ):
                terms = dot(lhs[...], rhs, 1, 1)
                if factor is not None:
                    terms = terms * factor
                acc[head, member, 0 : 2 * BLOCK] += terms[0 : 2 * BLOCK]
                targets = [outer_row] + [
                    3 + 2 * level + chosen(block, level) for level in range(LEVELS)
                ]
                for slot, row in enumerate(targets):
                    at = pl.ds(pl.multiple_of(row * BLOCK, BLOCK), BLOCK)
                    first = (2 + slot) * BLOCK
                    acc[head, member, at] += terms[first : first + BLOCK]
        for member in range(2):
            ext_store[head, member] = acc[head, member, 2 * BLOCK : 3 * BLOCK].astype(BF16)
            for level in range(LEVELS):
                first = (3 + 2 * level) * BLOCK
                level_store[head, level, member] = acc[
                    head, member, first : first + 2 * BLOCK
                ].astype(BF16)
        for copy in out_copies(head):
            copy.start()
        return carry

    lax.fori_loop(0, PER, one_head, 0)
    for head in range(PER):
        for copy in out_copies(head):
            copy.wait()


def attend_scratch(rows):
    return [
        pltpu.VMEM((SLOTS * BLOCK, ROWS), F32),
        pltpu.VMEM((SLOTS * BLOCK, ROWS), BF16),
        pltpu.VMEM((SLOTS * BLOCK, ROWS), BF16),
        pltpu.VMEM((2 * PER, 2, SLOTS * BLOCK, HEAD_DIM), BF16),
        pltpu.VMEM((PER, 2, 1040, HEAD_DIM), BF16),
        pltpu.VMEM((PER, 2, 1024, HEAD_DIM), BF16),
        pltpu.VMEM((PER, 2, (3 + 2 * LEVELS) * BLOCK, HEAD_DIM), F32),
        pltpu.VMEM((PER, 2, BLOCK, HEAD_DIM), BF16),
        pltpu.VMEM((PER, LEVELS, 2, rows, HEAD_DIM), BF16),
        pltpu.SemaphoreType.DMA((2 * PER,)),
        pltpu.SemaphoreType.DMA((PER, 2)),
        pltpu.SemaphoreType.DMA((PER, 4 + LEVELS)),
    ]


def finish_sides_kernel(scalars, *refs):
    sources, targets = refs[:-2], refs[-2:]
    order = query_order(scalars[0], 1)
    for member, target in enumerate(targets):
        for part in range(16):
            block, inner = part // 8, (part % 8) * 16
            pieces = []
            for head in range(2 * LOCAL_HEADS):
                local = head % LOCAL_HEADS
                source = sources[(head // LOCAL_HEADS) * CHUNKS + local // PER]
                for group in range(2):
                    start = (member * 2 + block) * 256 + group * 128 + inner
                    pieces.append(source[local % PER, start : start + 16])
            rows = jnp.concatenate(pieces, axis=0)
            target[part * 256 : part * 256 + 256] = dot(order, rows, 1, 0).astype(BF16)


def finish_pairs_kernel(scalars, *refs):
    even = scalars[0] == 0
    count = (len(refs) - 3) // 2
    far, targets, ins, sems = refs[:count], refs[count : count + 2], refs[count + 2 : -1], refs[-1]
    copies = [
        pltpu.make_async_copy(source, store, sems.at[i])
        for i, (source, store) in enumerate(zip(far, ins))
    ]
    for copy in copies:
        copy.start()
    for copy in copies:
        copy.wait()
    beyond, whole, split = ins[0], ins[1:4], ins[4:]
    order = key_order(1)
    for member, target in enumerate(targets):
        for part in range(4):
            span = slice(part * 64, part * 64 + 64)
            inner = slice((part % 2) * 64, (part % 2) * 64 + 64)
            pieces = []
            for head in range(LOCAL_HEADS):
                total = beyond[head, member, inner].astype(F32)
                total = jnp.where(even if part < 2 else jnp.logical_not(even), total, 0.0)
                for ref in whole:
                    total = total + ref[head, member, span].astype(F32)
                for ref in split[head // PER :: CHUNKS]:
                    total = total + ref[head % PER, member, span].astype(F32)
                pieces.append(total.astype(BF16))
            rows = jnp.concatenate(pieces, axis=0)
            target[part * 256 : part * 256 + 256] = dot(order, rows, 1, 0).astype(BF16)


def flipped(value, mask):
    return lax.ppermute(value, "seq", [(i, i ^ mask) for i in range(lax.axis_size("seq"))])


def past_end(value):
    pairs = []
    for i in range(1, lax.axis_size("seq") - 1, 2):
        pairs += [(i, i + 1), (i + 1, i)]
    return lax.ppermute(value, "seq", pairs)


def other_head(value):
    return lax.ppermute(value, "head", [(0, 1), (1, 0)])


def added(first, second):
    return (first.astype(F32) + second.astype(F32)).astype(BF16)


def shards(query, key_in, value, grad_out, band_width, stride_bits, partner_table):
    rows = key_in.shape[0]
    device = lax.axis_index("seq").astype(jnp.int32)
    place = lax.axis_index("head").astype(jnp.int32)
    odd = device & 1
    match = (stride_bits[None, :] == jnp.arange(LEVELS, dtype=jnp.int32)[:, None]).astype(jnp.int32)
    chosen = jnp.sum(partner_table[:, None, :] * match[None], axis=2)
    scalars = jnp.concatenate(
        [device[None], jnp.full((1,), lax.axis_size("seq") - 1, jnp.int32), chosen.reshape(-1)]
    )

    whole = jax.ShapeDtypeStruct((LOCAL_HEADS, 2, rows, HEAD_DIM), BF16)
    pair = jax.ShapeDtypeStruct((PER, 2, rows, HEAD_DIM), BF16)
    padded = jax.ShapeDtypeStruct((PER, 2, rows + PAD, HEAD_DIM), BF16)
    terms = jax.ShapeDtypeStruct((PER, 2, rows, HEAD_DIM), F32)
    ends = jax.ShapeDtypeStruct((LOCAL_HEADS, 2, BLOCK, HEAD_DIM), BF16)
    sides = jax.ShapeDtypeStruct((PER, 1040, HEAD_DIM), BF16)
    half = jax.ShapeDtypeStruct((PER, 1024, HEAD_DIM), BF16)

    own, own_a, own_b, own_end = pl.pallas_call(
        pack_pairs_kernel,
        out_shape=[whole, padded, padded, ends],
        in_specs=[SCALARS] + [FAR] * 2,
        out_specs=[WHOLE] * 4,
        scratch_shapes=[pltpu.VMEM((rows * 4, HEAD_DIM), BF16)] * 2
        + [pltpu.SemaphoreType.DMA((2, 2))],
        compiler_params=vmem(PACK_MIB),
        name="pack_pairs",
    )(odd[None], key_in.reshape(-1, HEAD_DIM), value.reshape(-1, HEAD_DIM))

    z2_a = flipped(own_a, 32)
    z1_a = flipped(own_a, 16)
    y1 = flipped(own, 2)
    core = flipped(own, 1)
    x = flipped(own, 8)
    ext = past_end(lax.optimization_barrier((own_end, core))[0])
    keep_a, keep_b, send_a, send_b = pl.pallas_call(
        pack_sides_kernel,
        out_shape=[sides] * (2 * CHUNKS),
        in_specs=[SCALARS] + [FAR] * 3,
        out_specs=[WHOLE] * (2 * CHUNKS),
        scratch_shapes=[pltpu.VMEM((rows * 16, HEAD_DIM), BF16)] * 2
        + [pltpu.SemaphoreType.DMA((2, 4))],
        compiler_params=vmem(SIDES_MIB),
        name="pack_sides",
    )(
        jnp.concatenate([place[None], band_width.reshape(-1)]),
        query.reshape(-1, HEAD_DIM),
        grad_out.reshape(-1, HEAD_DIM),
        core,
    )
    to_z2, to_head = lax.optimization_barrier((own_b, send_a))
    z6_a = flipped(z2_a, 96)
    z2_b = flipped(to_z2, 32)
    other_a = other_head(to_head)
    y3 = flipped(y1, 6)
    to_head, to_z1 = lax.optimization_barrier((send_b, to_z2))
    z4_b = flipped(to_z1, 64)
    z1_b = flipped(to_z1, 16)
    other_b = other_head(to_head)

    def attend(chunk, mine, keep, other, z1, z2, z4, reused):
        ins = [scalars, mine, ext, core, y1, y3, x, z1, z2, z4, keep, other, *reused]
        outs = [half, half, terms, ends, *[whole] * 4, padded, padded, padded]
        return pl.pallas_call(
            functools.partial(attend_kernel, chunk * PER, len(reused)),
            out_shape=outs,
            in_specs=[SCALARS] + [FAR] * (len(ins) - 1),
            out_specs=[FAR] * len(outs),
            scratch_shapes=attend_scratch(rows),
            input_output_aliases={12 + i: 3 + i for i in range(len(reused))},
            compiler_params=vmem(ATT_MIB),
            cost_estimate=pl.CostEstimate(
                flops=PER * 2 * 12 * SLOTS * BLOCK * ROWS * HEAD_DIM,
                transcendentals=PER * 2 * SLOTS * BLOCK * ROWS,
                bytes_accessed=PER * 24 * rows * HEAD_DIM * 4,
            ),
            name="attend",
        )(*ins)

    first = attend(0, own_a, keep_a, other_a, z1_a, z2_a, z6_a, [])
    keep_out_a, other_out_a, terms_a = first[:3]
    z1_terms_a, z2_terms_a, z4_terms_a = first[8:]
    far_a = flipped(z4_terms_a, 96)
    swapped_a = other_head(other_out_a)
    back_z1_a = flipped(z1_terms_a, 16)
    second = attend(1, own_b, keep_b, other_b, z1_b, z2_b, z4_b, first[3:8])
    keep_out_b, other_out_b, terms_b, ext_terms, core_terms, y1_terms, y2_terms = second[:7]
    x_terms, z1_terms_b, z2_terms_b, z4_terms_b = second[7:]
    to_z6, to_y3, to_head, to_ext, to_core, far_a, swapped_a, back_z1_a = lax.optimization_barrier(
        (z4_terms_b, y2_terms, other_out_b, ext_terms, core_terms, far_a, swapped_a, back_z1_a)
    )
    far_b = flipped(to_z6, 96)
    back_z2_a = flipped(added(z2_terms_a, far_a), 32)
    near = flipped(to_y3, 6)
    back_core = flipped(to_core, 1)
    swapped_b = other_head(to_head)
    back_ext = past_end(lax.optimization_barrier((to_ext, back_core))[0])
    far_b, back_z2_a, near, swapped_b, back_ext, z1_terms_b, x_terms = lax.optimization_barrier(
        (far_b, back_z2_a, near, swapped_b, back_ext, z1_terms_b, x_terms)
    )
    back_z2_b = flipped(added(z2_terms_b, far_b), 32)
    back_y = flipped(added(y1_terms, near), 2)
    back_x = flipped(x_terms, 8)
    back_z1_b = flipped(z1_terms_b, 16)

    out, dquery = pl.pallas_call(
        finish_sides_kernel,
        out_shape=[jax.ShapeDtypeStruct((rows * 16, HEAD_DIM), BF16)] * 2,
        in_specs=[SCALARS] + [WHOLE] * (2 * CHUNKS),
        out_specs=[WHOLE] * 2,
        compiler_params=vmem(8),
        name="finish_sides",
    )(place[None], keep_out_a, keep_out_b, swapped_a, swapped_b)
    sums = [back_ext, back_core, back_y, back_x, terms_a, terms_b]
    sums += [back_z1_a, back_z1_b, back_z2_a, back_z2_b]
    dkey, dvalue = pl.pallas_call(
        finish_pairs_kernel,
        out_shape=[jax.ShapeDtypeStruct((rows * 4, HEAD_DIM), BF16)] * 2,
        in_specs=[SCALARS] + [FAR] * len(sums),
        out_specs=[WHOLE] * 2,
        scratch_shapes=[pltpu.VMEM(part.shape, part.dtype) for part in sums]
        + [pltpu.SemaphoreType.DMA((len(sums),))],
        compiler_params=vmem(16),
        name="finish_pairs",
    )(odd[None], *sums)
    return (
        out.reshape(query.shape),
        dquery.reshape(query.shape),
        dkey.reshape(key_in.shape),
        dvalue.reshape(key_in.shape),
    )


def solution(mesh):
    placed = (
        P("seq", None, "head", None),
        P("seq", "head", None),
        P("seq", "head", None),
        P("seq", None, "head", None),
        P(None, "head"),
        P(),
        P("seq", None),
    )
    return jax.shard_map(
        shards,
        mesh=mesh,
        in_specs=placed,
        out_specs=(
            P("seq", None, "head", None),
            P("seq", None, "head", None),
            P("seq", "head", None),
            P("seq", "head", None),
        ),
        check_vma=False,
    )
```
